32 devices in a mesh: groups: 2 (over x), leaf: 16 (over z, y, core).
Axes of the slice: x: 2, y: 2, z: 4, core: 2. Of those that a mesh axis runs over, the one named last changes fastest.
Arguments:
- right_side: float32 [65536, 256], P(('groups', 'leaf')), parts along dimension 0, may hold values from -6 to 6
- cotangent: float32 [65536, 256], P(('groups', 'leaf')), parts along dimension 0, may hold values from -6 to 6
- coeff_basis: float32 [4, 64, 65536], P(None, None, ('groups', 'leaf')), parts along dimension 2, may hold values from -1 to 1
- saved_basis: float32 [4, 64, 65536], P(None, None, ('groups', 'leaf')), parts along dimension 2, may hold values from -0.24 to 0.24
- node_inverse: float32 [30, 128, 128], P('groups'), parts along dimension 0, may hold values from -1 to 2.5
- leaf_rows: int32 [32], P(('groups', 'leaf')), parts along dimension 0, may hold values from 1 to 2048, 24576 in all
Outputs:
- solution: float32 [65536, 256], P(('groups', 'leaf')), parts along dimension 0
- grad_left: bfloat16 [4, 64, 65536], P(None, None, ('groups', 'leaf')), parts along dimension 2
- grad_right: bfloat16 [4, 64, 65536], P(None, None, ('groups', 'leaf')), parts along dimension 2
The draws below stay inside these ranges and needn't reach their ends.
There are 2 independent parts, one for each index of `groups`. The reference program is written for one: setup_inputs(seed, part) draws one part's arguments, and reference() takes and returns one part's arrays. A program takes and returns all parts, laid end to end along the dimension named above; each array names one. Nothing has to cross between parts.
Inputs may be any that keep to these rules, and one draw needn't show every extreme that they name: `leaf_rows`: every leaf has at least one live row; the live rows of all leaves sum to 24576, and some leaf has all 2048 rows live.
All inputs are finite; a program needn't handle non-finite values. No bound on the sum of `leaf_rows` on one device may be relied on, other than what follows from the above.
Results may differ from the reference program's by a relative error of at most 0.001.
Values sent between devices are 32-bit elements; how exact they have to be, the bound alone decides.
A program may use at most 64 MiB of HBM per device.

```python
import math
import jax
import jax.numpy as jnp
import numpy as np
from jax import lax

RANK = 64
COLS = 256
ROWS_DEV = 2048
LEVELS = 4
NODES = 15
SIDE0 = 1
N_ROWS = 32768
N_LEAF = 16


def draw_coeff_basis(key, part):
    level_scale = 1.0 / jnp.sqrt(ROWS_DEV * SIDE0 * 2.0 ** jnp.arange(LEVELS, dtype=jnp.float32))
    sample = jnp.clip(jax.random.normal(key, (LEVELS, RANK, N_ROWS), jnp.float32), -4.0, 4.0)
    return sample * level_scale[:, None, None]


def draw_node_inverse(key, part):
    order_two = 2 * RANK
    identity = jnp.eye(order_two, dtype=jnp.float32)
    first_key = jax.random.fold_in(key, 11)
    spread_part = jnp.clip(jax.random.normal(first_key, (NODES, order_two, order_two), jnp.float32), -4.0, 4.0)
    diag_gain = jnp.ones((NODES, order_two), jnp.float32)
    return identity[None] * diag_gain[:, :, None] + spread_part * (0.5 / jnp.sqrt(jnp.float32(order_two)))


def levels(stream_key, shape, pieces, smallest, top_value):
    factor_of = 1.0
    for dim, parts in pieces:
        heights = jax.random.uniform(jax.random.fold_in(jax.random.fold_in(stream_key, 6), dim), (parts,), jnp.float32, smallest / len(pieces), top_value / len(pieces))
        factor_of = factor_of * jnp.repeat(jnp.exp(heights), shape[dim] // parts).reshape((-1,) + (1,) * (len(shape) - 1 - dim))
    return factor_of


def length_profile(number_of, total, bound, slope):
    loads = [(1 << 20) // math.isqrt(grade ** slope) + 1 for grade in range(2, number_of + 1)]
    surplus, holding = total - bound - (number_of - 1), [1] * (number_of - 1)
    while surplus > 0:
        free = [i for i in range(number_of - 1) if holding[i] < bound]
        whole, budget = sum([loads[i] for i in free]), surplus
        for i in free:
            extra = min(bound - holding[i], max(1, budget * loads[i] // whole), surplus)
            holding[i] = holding[i] + extra
            surplus = surplus - extra
    return np.array([bound] + holding)


def uneven_parts(stream_key, amount, total, bound, skew):
    if amount == 2:
        one = jax.random.randint(stream_key, (), max(1, total - bound), min(bound, total - 1) + 1)
        return jnp.stack([one, total - one])
    sizes = jnp.asarray(length_profile(amount, total, bound, skew), jnp.int32)
    pairs = (amount - 1) // 2
    donor, sink = sizes[1:1 + 2 * pairs:2], sizes[2:2 + 2 * pairs:2]
    slack = jnp.minimum(donor - 1, bound - sink)
    shifted = jax.random.randint(jax.random.fold_in(stream_key, 1), (pairs,), 0, 1 << 20) % (slack + 1)
    sizes = sizes.at[1:1 + 2 * pairs:2].set(donor - shifted).at[2:2 + 2 * pairs:2].set(sink + shifted)
    return sizes[jax.random.permutation(jax.random.fold_in(stream_key, 2), amount)]


def normal_values(key, shape, scale, bound, pieces=(), kind=jnp.bfloat16):
    entries = jax.random.normal(key, shape, jnp.float32) * scale
    if len(pieces) > 0:
        entries = levels(key, shape, pieces, -0.22, 0.18) * entries
    return jnp.clip(entries, min=-bound, max=bound).astype(kind)


def setup_inputs(seed: int = 0, part: int = 0) -> dict:
    streams_of = jax.random.split(jax.random.key(seed), 7)
    own_keys = jax.random.split(jax.random.fold_in(streams_of[6], part), 7)
    right_side = normal_values(own_keys[0], (N_ROWS, COLS), 1.0, 6.0, ((0, 16),), jnp.float32)
    cotangent = normal_values(own_keys[1], (N_ROWS, COLS), 1.0, 6.0, ((0, 16),), jnp.float32)
    coeff_basis = draw_coeff_basis(jax.random.fold_in(jax.random.fold_in(streams_of[6], part), 71), part)
    saved_basis = normal_values(own_keys[3], (LEVELS, RANK, N_ROWS), 0.04, 0.24, ((2, 16),), jnp.float32)
    node_inverse = draw_node_inverse(jax.random.fold_in(jax.random.fold_in(streams_of[6], part), 71), part)
    leaf_rows = uneven_parts(own_keys[5], N_LEAF, N_LEAF * ROWS_DEV * 3 // 4, ROWS_DEV, 1).astype(jnp.int32)
    return {"right_side": right_side, "cotangent": cotangent, "coeff_basis": coeff_basis, "saved_basis": saved_basis, "node_inverse": node_inverse, "leaf_rows": leaf_rows}


def reference(right_side, cotangent, coeff_basis, saved_basis, node_inverse, leaf_rows):
    highest = lax.Precision.HIGHEST
    row_count = right_side.shape[0]
    within = jnp.arange(row_count, dtype=jnp.int32) % ROWS_DEV
    live_rows = (within < jnp.repeat(leaf_rows, ROWS_DEV)).astype(jnp.float32)
    current = right_side * live_rows[:, None]
    weights = cotangent * live_rows[:, None]
    saved_masked = saved_basis * live_rows[None, None, :]
    for height in range(LEVELS):
        side_count = 2 ** (LEVELS - height)
        side_rows = row_count // side_count
        basis_now = coeff_basis[height].reshape(RANK, side_count, side_rows)
        blocks = current.reshape(side_count, side_rows, COLS)
        coeffs = jnp.einsum('rsi,sic->src', basis_now, blocks, precision=highest)
        paired = coeffs.reshape(side_count // 2, 2 * RANK, COLS)
        offset = 2 ** LEVELS - side_count
        inverse = node_inverse[offset:offset + side_count // 2]
        mixture = jnp.einsum('nab,nbc->nac', inverse, paired, precision=highest).reshape(side_count, RANK, COLS)
        correction = jnp.einsum('rsi,src->sic', saved_masked[height].reshape(RANK, side_count, side_rows), mixture, precision=highest)
        current = current - correction.reshape(row_count, COLS)
    scale_factor = 1.0 / jnp.sqrt(jnp.float32(COLS))
    left_list = []
    right_list = []
    for height in range(LEVELS):
        side_count = 2 ** (LEVELS - height)
        side_rows = row_count // side_count
        basis_now = coeff_basis[height].reshape(RANK, side_count, side_rows)
        wblocks = weights.reshape(side_count, side_rows, COLS)
        fblocks = current.reshape(side_count, side_rows, COLS)
        k_sums = jnp.einsum('rsi,sic->src', basis_now, wblocks, precision=highest)
        l_sums = jnp.einsum('rsi,sic->src', basis_now, fblocks, precision=highest)
        k_swap = k_sums.reshape(side_count // 2, 2, RANK, COLS)[:, ::-1].reshape(side_count, RANK, COLS)
        l_swap = l_sums.reshape(side_count // 2, 2, RANK, COLS)[:, ::-1].reshape(side_count, RANK, COLS)
        left_now = jnp.einsum('src,sic->rsi', l_swap, wblocks, precision=highest) * scale_factor
        right_now = jnp.einsum('src,sic->rsi', k_swap, fblocks, precision=highest) * scale_factor
        left_list.append(left_now.reshape(RANK, row_count))
        right_list.append(right_now.reshape(RANK, row_count))
    grad_left = jnp.stack(left_list).astype(jnp.bfloat16)
    grad_right = jnp.stack(right_list).astype(jnp.bfloat16)
    return (current, grad_left, grad_right)
```

```python
import functools
import math

import jax
import jax.numpy as jnp
from jax import lax
from jax.experimental import pallas as pl
from jax.experimental.pallas import tpu as pltpu
from jax.sharding import PartitionSpec as P

MESH = pl.DeviceIdType.MESH
TILE = 512
VMEM_TREE = 32 * 2**20
VMEM_FINISH = 16 * 2**20


def swapped(value, bit):
    mask = 2**bit
    pairs = [(source, source ^ mask) for source in range(lax.axis_size("leaf"))]
    return lax.ppermute(value, "leaf", pairs)


def dot(a, b, dims=((1,), (0,))):
    return triple(split(a), split(b), dims)


def tree_kernel(
    levels, rank, base, s_ref, k_ref, g_ref, node_ref, z_out, l_out, k_out, *scratch
):
    steps = [lambda: None] * 3
    tree_steps(
        levels, rank, base, steps, s_ref, k_ref, g_ref, node_ref, z_out, l_out, k_out, scratch
    )


def whole_kernel(
    levels,
    rank,
    tile,
    rows_ref,
    right_ref,
    cot_ref,
    basis_ref,
    saved_ref,
    node_ref,
    z_out,
    l_out,
    k_out,
    right_out,
    cot_high,
    cot_low,
    saved_high,
    saved_low,
    s_ref,
    k_ref,
    g_ref,
    right_in,
    cot_in,
    basis_in,
    saved_in,
    high_ref,
    low_ref,
    load_sem,
    *scratch,
):
    tiles = basis_ref.shape[1] // tile

    def load(source, target, kind, axis):
        copies = []
        for n in range(tiles):
            part = pl.ds(n * tile, tile)
            index = (part, slice(None)) if axis == 0 else (slice(None), part)
            copies.append(
                pltpu.make_async_copy(source.at[index], target.at[index], load_sem.at[kind, n])
            )
        return copies

    basis_loads = load(basis_ref, basis_in, 0, 1)
    saved_loads = load(saved_ref, saved_in, 1, 1)
    right_loads = load(right_ref, right_in, 2, 0)
    cot_loads = load(cot_ref, cot_in, 3, 0)
    for one, two in zip(basis_loads, saved_loads):
        one.start()
        two.start()
    for one in right_loads + cot_loads:
        one.start()

    def gram_step():
        total = None
        for n in range(tiles):
            part = slice(n * tile, (n + 1) * tile)
            live = n * tile + lax.broadcasted_iota(jnp.int32, (1, tile), 1) < rows_ref[0]
            basis_loads[n].wait()
            high, low = split(jnp.where(live, basis_in[:, part], 0.0))
            high_ref[:, part] = high
            low_ref[:, part] = low
            saved_loads[n].wait()
            saved = split(jnp.where(live, saved_in[:, part], 0.0))
            saved_high[:, part], saved_low[:, part] = saved
            term = triple((high, low), saved, ((1,), (1,)))
            total = term if total is None else total + term
        g_ref[...] = total

    def column_step(loads, source, target, keep):
        for n in range(tiles):
            loads[n].wait()
        total = None
        for n in range(tiles):
            part = slice(n * tile, (n + 1) * tile)
            live = n * tile + lax.broadcasted_iota(jnp.int32, (tile, 1), 0) < rows_ref[0]
            value = jnp.where(live, source[part, :], 0.0)
            pair = split(value)
            keep(part, value, pair)
            basis = (high_ref[:, part], low_ref[:, part])
            term = triple(basis, pair, ((1,), (0,)))
            total = term if total is None else total + term
        target[...] = total

    def keep_right(part, value, pair):
        right_out[part, :] = value

    def keep_cot(part, value, pair):
        cot_high[part, :], cot_low[part, :] = pair

    steps = [
        gram_step,
        lambda: column_step(right_loads, right_in, s_ref, keep_right),
        lambda: column_step(cot_loads, cot_in, k_ref, keep_cot),
    ]
    tree_steps(
        levels, rank, 0, steps, s_ref, k_ref, g_ref, node_ref, z_out, l_out, k_out, scratch
    )


def tree_steps(
    levels, rank, base, steps, s_ref, k_ref, g_ref, node_ref, z_out, l_out, k_out, scratch
):
    inverse = scratch[0]
    own = [None] + [scratch[1 + 3 * n : 4 + 3 * n] for n in range(levels - 1)]
    start = 1 + 3 * (levels - 1)
    got = [scratch[start + 3 * n : start + 3 * n + 3] for n in range(levels)]
    start += 3 * levels
    packed, other, node_sem, send_sem, recv_sem = scratch[start:]
    cols = s_ref.shape[1]
    half = cols // 2
    position = lax.axis_index("leaf")

    def bit_of(height):
        return lax.rem(lax.div(position, 2 ** (base + height)), 2)

    def partner(height):
        return position + (1 - 2 * bit_of(height)) * 2 ** (base + height)

    fetches = []
    for height in range(levels):
        offset = 2**levels - 2 ** (levels - height)
        node = offset + lax.div(position, 2 ** (base + height + 1))
        fetch = pltpu.make_async_copy(node_ref.at[node], inverse.at[height], node_sem.at[height])
        fetch.start()
        fetches.append(fetch)

    barrier = pltpu.get_barrier_semaphore()
    for height in range(levels):
        pl.semaphore_signal(
            barrier, inc=1, device_id={"leaf": partner(height)}, device_id_type=MESH
        )
    steps[0]()
    pl.semaphore_wait(barrier, levels)

    def send(source, target, height, slot):
        copy = pltpu.make_async_remote_copy(
            src_ref=source,
            dst_ref=target,
            send_sem=send_sem.at[slot],
            recv_sem=recv_sem.at[slot],
            device_id={"leaf": partner(height)},
            device_id_type=MESH,
        )
        copy.start()
        return copy

    mine = bit_of(0)
    keep = pl.ds(pl.multiple_of(mine * half, half), half)
    give = pl.ds(pl.multiple_of((1 - mine) * half, half), half)
    s_all = [s_ref.at[:, keep]] + [own[n][0] for n in range(1, levels)]
    g_all = [g_ref] + [own[n][1] for n in range(1, levels)]
    k_all = [k_ref.at[:, keep]] + [own[n][2] for n in range(1, levels)]
    sends = []

    def half_rows(height):
        size = g_all[height].shape[0] // 2
        return pl.ds(pl.multiple_of(mine * size, 8), size)

    def advance_gram(height, copy):
        copy.wait_recv()
        if 0 < height < levels - 1:
            area = got[height][1].at[half_rows(height), :]
            relay = send(area, area, 0, 3 * levels + 2 + height)
            sends.append(relay)
            relay.wait_recv()
        if height == levels - 1:
            return None
        g_now, g_got, g_next = g_all[height], got[height][1], g_all[height + 1]
        skip = g_now.shape[1] - g_next.shape[1]
        g_next[...] = g_now[rank:, skip:] + g_got[rank:, skip:]
        source, target = g_next, got[height + 1][1]
        if height < levels - 2:
            area = half_rows(height + 1)
            source, target = source.at[area, :], target.at[area, :]
        sends.append(send(source, target, height + 1, 3 * height + 4))
        return sends[-1]

    g_copy = send(g_ref, got[0][1], 0, 1)
    sends.append(g_copy)
    steps[1]()
    s_copy = send(s_ref.at[:, give], got[0][0], 0, 0)
    sends.append(s_copy)
    g_copy = advance_gram(0, g_copy)
    steps[2]()
    k_copy = send(k_ref.at[:, give], got[0][2], 0, 2)
    sends.append(k_copy)
    z_own, z_sib = [], []
    for height in range(levels):
        shift = rank * height - rank * height // 128 * 128
        s_now, g_now, k_now = s_all[height], g_all[height], k_all[height]
        s_got, g_got, k_got = got[height]
        s_copy.wait_recv()
        lower = bit_of(height) == 0
        here, there = s_now[:rank, :], s_got[:rank, :]
        pair = jnp.concatenate(
            [jnp.where(lower, here, there), jnp.where(lower, there, here)], 0
        )
        fetches[height].wait()
        z = dot(inverse[height], pair)
        z_own.append(jnp.where(lower, z[:rank], z[rank:]))
        z_sib.append(jnp.where(lower, z[rank:], z[:rank]))
        if height < levels - 1:
            s_next, _, k_next = own[height + 1]
            block = slice(shift, shift + rank)
            s_next[...] = (
                s_now[rank:, :]
                + s_got[rank:, :]
                - dot(g_now[rank:, :][:, block], z_own[-1])
                - dot(g_got[rank:, :][:, block], z_sib[-1])
            )
            s_copy = send(s_next, got[height + 1][0], height + 1, 3 * height + 3)
            sends.append(s_copy)
            k_copy.wait_recv()
            k_next[...] = k_now[rank:, :] + k_got[rank:, :]
            k_copy = send(k_next, got[height + 1][2], height + 1, 3 * height + 5)
            sends.append(k_copy)
            g_copy = advance_gram(height + 1, g_copy)
    rows = levels * rank
    scale = 1.0 / math.sqrt(cols)
    z_all = jnp.concatenate(z_own, 0)
    areas = [pl.ds(n * rows, rows) for n in range(3)]
    packed[:rank, :] = z_sib[0]
    packed[rank:rows, :] = z_all[rank:]
    last = [send(packed.at[areas[0]], other.at[areas[0]], 0, 3 * levels)]
    z_out[:, keep] = z_all
    l_first = (s_ref[:rank, keep] - dot(g_ref[:rank, :], z_all)) * scale
    packed[rows : rows + rank, :] = l_first
    for height in range(levels):
        shift = rank * height - rank * height // 128 * 128
        part = slice(height * rank, (height + 1) * rank)
        chain = jnp.concatenate([z_sib[height]] + z_own[height + 1 :], 0)
        row = got[height][1][:rank, :][:, shift:]
        l_part = (got[height][0][:rank, :] - dot(row, chain)) * scale
        l_out[part, keep] = l_part
        if height > 0:
            packed[rows + height * rank : rows + (height + 1) * rank, :] = l_part
    last.append(send(packed.at[areas[1]], other.at[areas[1]], 0, 3 * levels + 1))
    k_copy.wait_recv()
    packed[2 * rows : 2 * rows + rank, :] = k_ref[:rank, keep] * scale
    for height in range(levels):
        part = slice(height * rank, (height + 1) * rank)
        k_part = got[height][2][:rank, :] * scale
        k_out[part, keep] = k_part
        if height > 0:
            packed[2 * rows + height * rank : 2 * rows + (height + 1) * rank, :] = k_part
    last.append(send(packed.at[areas[2]], other.at[areas[2]], 0, 3 * levels + 2))
    for copy, target, area in zip(last, (z_out, l_out, k_out), areas):
        copy.wait_recv()
        target[:, give] = other[area, :]
    for copy in sends + last:
        copy.wait_send()


def tree_scratch(levels, rank, rows, cols, node_shape):
    half = cols // 2
    own, got = [], []
    for height in range(levels):
        left = rows - rank * height
        wide = rows - rank * height // 128 * 128
        group = [
            pltpu.VMEM((left, half), jnp.float32),
            pltpu.VMEM((left, wide), jnp.float32),
            pltpu.VMEM((left, half), jnp.float32),
        ]
        got += group
        if height > 0:
            own += group
    count = 4 * levels + 1
    return (
        [pltpu.VMEM((levels,) + node_shape, jnp.float32)]
        + own
        + got
        + [
            pltpu.VMEM((3 * rows, half), jnp.float32),
            pltpu.VMEM((3 * rows, half), jnp.float32),
            pltpu.SemaphoreType.DMA((levels,)),
            pltpu.SemaphoreType.DMA((count,)),
            pltpu.SemaphoreType.DMA((count,)),
        ]
    )


def tree(sums, weight_sums, gram, node_inverse, levels, rank, base):
    rows, cols = sums.shape
    vmem = pl.BlockSpec(memory_space=pltpu.VMEM)
    return pl.pallas_call(
        functools.partial(tree_kernel, levels, rank, base),
        out_shape=[jax.ShapeDtypeStruct((rows, cols), jnp.float32)] * 3,
        in_specs=[vmem] * 3 + [pl.BlockSpec(memory_space=pl.ANY)],
        out_specs=[vmem] * 3,
        scratch_shapes=tree_scratch(levels, rank, rows, cols, node_inverse.shape[1:]),
        compiler_params=pltpu.CompilerParams(collective_id=0, has_side_effects=True),
    )(sums, weight_sums, gram, node_inverse)


def whole_tree(leaf_rows, right_side, cotangent, basis, saved, node_inverse, levels, rank, tile):
    rows, depth = basis.shape
    cols = right_side.shape[1]
    vmem = pl.BlockSpec(memory_space=pltpu.VMEM)
    hbm = pl.BlockSpec(memory_space=pltpu.HBM)
    args = (right_side, cotangent, basis, saved, node_inverse)
    shapes = (
        [((rows, cols), jnp.float32)] * 3
        + [((depth, cols), jnp.float32)]
        + [((depth, cols), jnp.bfloat16)] * 2
        + [((rows, depth), jnp.bfloat16)] * 2
    )
    return pl.pallas_call(
        functools.partial(whole_kernel, levels, rank, tile),
        out_shape=[pltpu.VMEM(shape, dtype) for shape, dtype in shapes],
        in_specs=[pl.BlockSpec(memory_space=pltpu.SMEM)] + [hbm] * 5,
        out_specs=[vmem] * 8,
        scratch_shapes=[
            pltpu.VMEM((rows, cols), jnp.float32),
            pltpu.VMEM((rows, cols), jnp.float32),
            pltpu.VMEM((rows, rows), jnp.float32),
            pltpu.VMEM((depth, cols), jnp.float32),
            pltpu.VMEM((depth, cols), jnp.float32),
            pltpu.VMEM((rows, depth), jnp.float32),
            pltpu.VMEM((rows, depth), jnp.float32),
            pltpu.VMEM((rows, depth), jnp.bfloat16),
            pltpu.VMEM((rows, depth), jnp.bfloat16),
            pltpu.SemaphoreType.DMA((4, depth // tile)),
        ]
        + tree_scratch(levels, rank, rows, cols, node_inverse.shape[1:]),
        compiler_params=pltpu.CompilerParams(
            collective_id=0, has_side_effects=True, vmem_limit_bytes=VMEM_TREE
        ),
    )(leaf_rows, *[pltpu.with_memory_space_constraint(arg, pltpu.HBM) for arg in args])


def finish_kernel(
    tile,
    z_ref,
    l_ref,
    k_ref,
    right_ref,
    cot_high,
    cot_low,
    saved_high,
    saved_low,
    x_hbm,
    left_hbm,
    grad_hbm,
    x_ref,
    left_ref,
    grad_ref,
    sem,
):
    tiles = right_ref.shape[0] // tile
    copies = []

    def out(source, target, index, kind, n):
        copy = pltpu.make_async_copy(source.at[index], target.at[index], sem.at[kind, n])
        copy.start()
        copies.append(copy)

    z, left, right = split(z_ref[...]), split(l_ref[...]), split(k_ref[...])
    for n in range(tiles):
        part = slice(n * tile, (n + 1) * tile)
        down, across = (part, slice(None)), (slice(None), part)
        moved = triple((saved_high[across], saved_low[across]), z, ((0,), (0,)))
        solved = right_ref[down] - moved
        x_ref[down] = solved
        out(x_ref, x_hbm, down, 0, n)
        value = triple(left, (cot_high[down], cot_low[down]), ((1,), (1,)))
        left_ref[across] = value.astype(jnp.bfloat16)
        out(left_ref, left_hbm, across, 1, n)
        value = triple(right, split(solved), ((1,), (1,)))
        grad_ref[across] = value.astype(jnp.bfloat16)
        out(grad_ref, grad_hbm, across, 2, n)
    for copy in copies:
        copy.wait()


def finish(parts, tile):
    right_side = parts[3]
    depth, cols = right_side.shape
    rows = parts[0].shape[0]
    vmem = pl.BlockSpec(memory_space=pltpu.VMEM)
    hbm = pl.BlockSpec(memory_space=pltpu.HBM)
    shapes = [
        ((depth, cols), jnp.float32),
        ((rows, depth), jnp.bfloat16),
        ((rows, depth), jnp.bfloat16),
    ]
    return pl.pallas_call(
        functools.partial(finish_kernel, tile),
        out_shape=[pltpu.HBM(shape, dtype) for shape, dtype in shapes],
        in_specs=[vmem] * 8,
        out_specs=[hbm] * 3,
        scratch_shapes=[pltpu.VMEM(shape, dtype) for shape, dtype in shapes]
        + [pltpu.SemaphoreType.DMA((3, depth // tile))],
        compiler_params=pltpu.CompilerParams(vmem_limit_bytes=VMEM_FINISH),
    )(*[pltpu.with_memory_space_constraint(part, pltpu.VMEM) for part in parts])


def split(value):
    high = value.astype(jnp.bfloat16)
    return high, (value - high.astype(jnp.float32)).astype(jnp.bfloat16)


def triple(left, right, dims):
    def one(a, b):
        return lax.dot_general(a, b, (dims, ((), ())), preferred_element_type=jnp.float32)

    return one(left[0], right[1]) + one(left[1], right[0]) + one(left[0], right[0])


def lead_kernel(rows_ref, right_ref, cot_ref, basis_ref, saved_ref, s_ref, k_ref, g_ref):
    step = pl.program_id(0)
    tile = basis_ref.shape[1]
    place = step * tile + lax.broadcasted_iota(jnp.int32, (1, tile), 1)
    basis = split(jnp.where(place < rows_ref[0], basis_ref[...], 0.0))
    s_now = triple(basis, split(right_ref[...]), ((1,), (0,)))
    k_now = triple(basis, split(cot_ref[...]), ((1,), (0,)))
    g_now = triple(basis, split(saved_ref[...]), ((1,), (1,)))

    @pl.when(step == 0)
    def _():
        s_ref[...] = s_now
        k_ref[...] = k_now
        g_ref[...] = g_now

    @pl.when(step > 0)
    def _():
        s_ref[...] += s_now
        k_ref[...] += k_now
        g_ref[...] += g_now


def close_kernel(
    rows_ref, right_ref, cot_ref, saved_ref, z_ref, l_ref, k_ref, x_ref, left_ref, grad_ref
):
    tile = saved_ref.shape[1]
    first = pl.program_id(0) * tile
    down = first + lax.broadcasted_iota(jnp.int32, (tile, 1), 0)
    across = first + lax.broadcasted_iota(jnp.int32, (1, tile), 1)
    moved = triple(split(saved_ref[...]), split(z_ref[...]), ((0,), (0,)))
    solved = jnp.where(down < rows_ref[0], right_ref[...] - moved, 0.0)
    x_ref[...] = solved
    left = triple(split(l_ref[...]), split(cot_ref[...]), ((1,), (1,)))
    left_ref[...] = jnp.where(across < rows_ref[0], left, 0.0).astype(jnp.bfloat16)
    grad = triple(split(k_ref[...]), split(solved), ((1,), (1,)))
    grad_ref[...] = grad.astype(jnp.bfloat16)


def body(right_side, cotangent, coeff_basis, saved_basis, node_inverse, leaf_rows):
    row_count, cols = right_side.shape
    levels, rank = coeff_basis.shape[0], coeff_basis.shape[1]
    height = levels * rank
    base = lax.axis_size("leaf").bit_length() - 1 - levels
    basis = coeff_basis.reshape(height, row_count)
    saved = saved_basis.reshape(height, row_count)
    tile = math.gcd(row_count, TILE)
    grid = (row_count // tile,)
    count = pl.BlockSpec(memory_space=pltpu.SMEM)
    tall = pl.BlockSpec((tile, cols), lambda i: (i, 0))
    wide = pl.BlockSpec((height, tile), lambda i: (0, i))
    small = pl.BlockSpec((height, cols), lambda i: (0, 0))
    square = pl.BlockSpec((height, height), lambda i: (0, 0))
    if base == 0:
        parts = whole_tree(
            leaf_rows, right_side, cotangent, basis, saved, node_inverse, levels, rank, tile
        )
        current, left, right = finish(parts, tile)
    else:
        sums, weight_sums, gram = pl.pallas_call(
            lead_kernel,
            grid=grid,
            out_shape=[
                jax.ShapeDtypeStruct((height, cols), jnp.float32),
                jax.ShapeDtypeStruct((height, cols), jnp.float32),
                jax.ShapeDtypeStruct((height, height), jnp.float32),
            ],
            in_specs=[count, tall, tall, wide, wide],
            out_specs=[small, small, square],
        )(leaf_rows, right_side, cotangent, basis, saved)
        for bit in range(base):
            sums = sums + swapped(sums, bit)
            weight_sums = weight_sums + swapped(weight_sums, bit)
            gram = gram + swapped(gram, bit)
        z_own, l_sib, k_sib = tree(sums, weight_sums, gram, node_inverse, levels, rank, base)
        current, left, right = pl.pallas_call(
            close_kernel,
            grid=grid,
            out_shape=[
                jax.ShapeDtypeStruct((row_count, cols), jnp.float32),
                jax.ShapeDtypeStruct((height, row_count), jnp.bfloat16),
                jax.ShapeDtypeStruct((height, row_count), jnp.bfloat16),
            ],
            in_specs=[count, tall, tall, wide, small, small, small],
            out_specs=[tall, wide, wide],
        )(leaf_rows, right_side, cotangent, saved, z_own, l_sib, k_sib)
    shape = (levels, rank, row_count)
    return current, left.reshape(shape), right.reshape(shape)


def solution(mesh):
    in_specs = (
        P(("groups", "leaf"), None),
        P(("groups", "leaf"), None),
        P(None, None, ("groups", "leaf")),
        P(None, None, ("groups", "leaf")),
        P("groups", None, None),
        P(("groups", "leaf")),
    )
    out_specs = (
        P(("groups", "leaf"), None),
        P(None, None, ("groups", "leaf")),
        P(None, None, ("groups", "leaf")),
    )
    return jax.shard_map(body, mesh=mesh, in_specs=in_specs, out_specs=out_specs, check_vma=False)
```

```python
import functools
import math

import jax
import jax.numpy as jnp
from jax import lax
from jax.experimental import pallas as pl
from jax.experimental.pallas import tpu as pltpu
from jax.sharding import PartitionSpec as P

MESH = pl.DeviceIdType.MESH
TILE = 512
SLOTS = 32
VMEM_TREE = 32 * 2**20
VMEM_FINISH = 16 * 2**20


def swapped(value, bit):
    mask = 2**bit
    pairs = [(source, source ^ mask) for source in range(lax.axis_size("leaf"))]
    return lax.ppermute(value, "leaf", pairs)


def dot(a, b, dims=((1,), (0,))):
    return triple(split(a), split(b), dims)


def tree_kernel(
    levels, rank, base, s_ref, k_ref, g_ref, node_ref, z_out, l_out, k_out, *scratch
):
    steps = [lambda: None] * 3
    tree_steps(
        levels, rank, base, steps, s_ref, k_ref, g_ref, node_ref, z_out, l_out, k_out, scratch
    )


def whole_kernel(
    levels,
    rank,
    tile,
    rows_ref,
    right_ref,
    cot_ref,
    basis_ref,
    saved_ref,
    node_ref,
    l_out,
    k_out,
    right_in,
    cot_high,
    cot_low,
    z_out,
    saved_high,
    saved_low,
    s_ref,
    k_ref,
    g_ref,
    g_got,
    cot_in,
    basis_in,
    saved_in,
    high_ref,
    low_ref,
    inverse,
    mix_high,
    mix_low,
    l_own,
    l_ship,
    k_ship,
    z_ship,
    load_sem,
    node_sem,
    send_sem,
    recv_sem,
    *scratch,
):
    depth = basis_ref.shape[1]
    rows, cols = s_ref.shape
    half = cols // 2
    last = levels - 1
    tiles = depth // tile
    scale = 1.0 / math.sqrt(cols)
    position = lax.axis_index("leaf")
    s_got, s_sum, k_got, k_sum = [list(scratch[levels * n : levels * (n + 1)]) for n in range(4)]
    sum_one, got_tail, got_head, sum_two, got_two, sum_three, got_three, near, far = scratch[4 * levels :]

    def bit_of(height):
        return lax.rem(lax.div(position, 2**height), 2)

    def partner(*heights):
        return position + sum((1 - 2 * bit_of(height)) * 2**height for height in heights)

    def block(level, base=0):
        return slice((level - base) * rank, (level - base + 1) * rank)

    def load(source, target, kind, axis):
        copies = []
        for n in range(tiles):
            part = pl.ds(n * tile, tile)
            index = (part, slice(None)) if axis == 0 else (slice(None), part)
            copies.append(
                pltpu.make_async_copy(source.at[index], target.at[index], load_sem.at[kind, n])
            )
        return copies

    basis_loads = load(basis_ref, basis_in, 0, 1)
    saved_loads = load(saved_ref, saved_in, 1, 1)
    right_loads = load(right_ref, right_in, 2, 0)
    cot_loads = load(cot_ref, cot_in, 3, 0)
    for one_load, two_load in zip(basis_loads, saved_loads):
        one_load.start()
        two_load.start()
    for one_load in right_loads + cot_loads:
        one_load.start()
    fetches = []
    for height in range(levels):
        offset = 2**levels - 2 ** (levels - height)
        node = offset + lax.div(position, 2 ** (height + 1))
        fetch = pltpu.make_async_copy(node_ref.at[node], inverse.at[height], node_sem.at[height])
        fetch.start()
        fetches.append(fetch)

    barrier = pltpu.get_barrier_semaphore()
    partners = [(height,) for height in range(levels)] + [(1, 2), (2, 3)]
    for heights in partners:
        pl.semaphore_signal(
            barrier, inc=1, device_id={"leaf": partner(*heights)}, device_id_type=MESH
        )

    sends = []

    def send(source, target, *heights):
        slot = len(sends)
        copy = pltpu.make_async_remote_copy(
            src_ref=source,
            dst_ref=target,
            send_sem=send_sem.at[slot],
            recv_sem=recv_sem.at[slot],
            device_id={"leaf": partner(*heights)},
            device_id_type=MESH,
        )
        copy.start()
        sends.append(copy)
        return copy

    mine = bit_of(0)
    keep = pl.ds(pl.multiple_of(mine * half, half), half)
    give = pl.ds(pl.multiple_of((1 - mine) * half, half), half)

    def gram_step():
        total = None
        for n in range(tiles):
            part = slice(n * tile, (n + 1) * tile)
            live = n * tile + lax.broadcasted_iota(jnp.int32, (1, tile), 1) < rows_ref[0]
            basis_loads[n].wait()
            high, low = split(jnp.where(live, basis_in[:, part], 0.0))
            high_ref[:, part] = high
            low_ref[:, part] = low
            saved_loads[n].wait()
            saved = split(saved_in[:, part])
            saved_high[:, part], saved_low[:, part] = saved
            term = triple(saved, (high, low), ((1,), (1,)))
            total = term if total is None else total + term
        g_ref[...] = total

    def column_step(loads, source, target, store):
        for one_load in loads:
            one_load.wait()
        total = None
        for n in range(tiles):
            part = slice(n * tile, (n + 1) * tile)
            pair = split(source[part, :])
            store(part, pair)
            term = triple((high_ref[:, part], low_ref[:, part]), pair, ((1,), (0,)))
            total = term if total is None else total + term
        target[...] = total

    def store_right(part, pair):
        pass

    def store_cot(part, pair):
        cot_high[part, :], cot_low[part, :] = pair

    lane = lax.broadcasted_iota(jnp.int32, (1, 2 * rank), 1)
    left_lanes = lane < rank

    def order(height, own, sibling):
        lower = bit_of(height) == 0
        return jnp.concatenate(
            [jnp.where(lower, own, sibling), jnp.where(lower, sibling, own)], 0
        )

    def prepare(height, own, sibling, part):
        fetches[height].wait()
        node = inverse[height]
        cross = dot(order(height, own, sibling), node, ((0,), (0,)))[part]
        high, low = split(jnp.concatenate([node, cross], 0))
        mix_high[: high.shape[0]] = high
        mix_low[: low.shape[0]] = low

    z_own, z_sib = [], []

    def solve(height, count):
        own = s_ref[:, keep] if height == 0 else s_sum[height][...]
        s_copies[0].wait_recv()
        pair = order(height, own[:rank], s_got[height][:rank, :])
        high, low = split(pair)
        size = 2 * rank + count
        wide = one(mix_high[:size], jnp.concatenate([high, low], 1))
        out = wide[:, :half] + wide[:, half:] + one(mix_low[:size], high)
        lower = bit_of(height) == 0
        z_own.append(jnp.where(lower, out[:rank], out[rank : 2 * rank]))
        z_sib.append(jnp.where(lower, out[rank : 2 * rank], out[:rank]))
        change = out[2 * rank :]
        if height < last:
            for copy in s_copies[1:]:
                copy.wait_recv()
            following = own[rank:] + s_got[height][rank:, :] - change
            s_sum[height + 1][...] = following
            target = s_got[height + 1]
            source = s_sum[height + 1]
            s_copies[:] = [send(source.at[:rank], target.at[:rank], height + 1)]
            if height + 1 < last:
                s_copies.append(send(source.at[rank:], target.at[rank:], height + 1))
        z_out[block(height), keep] = z_own[-1]
        z_ship[block(height)] = z_sib[-1] if height == 0 else z_own[-1]
        return change

    def one(a, b):
        return lax.dot_general(
            a, b, (((1,), (0,)), ((), ())), preferred_element_type=jnp.float32
        )

    def turned(a, b):
        return dot(a, b, ((0,), (0,)))

    def share(size):
        return pl.ds(pl.multiple_of(mine * size, 8), size)

    def relay(area):
        return send(area, area, 0)

    def move_early():
        z = split(z_out[: last * rank, :])
        for n in range(tiles):
            part = slice(n * tile, (n + 1) * tile)
            saved = (saved_high[: last * rank, part], saved_low[: last * rank, part])
            right_in[part, :] -= triple(saved, z, ((0,), (0,)))

    def move_late(columns):
        high, low = split(z_out[last * rank :, columns])
        stacked = jnp.concatenate([high, high, low], 0)
        for n in range(tiles):
            part = slice(n * tile, (n + 1) * tile)
            saved = saved_high[last * rank :, part]
            saved = jnp.concatenate([saved, saved_low[last * rank :, part], saved], 0)
            moved = lax.dot_general(
                saved, stacked, (((0,), (0,)), ((), ())), preferred_element_type=jnp.float32
            )
            live = n * tile + lax.broadcasted_iota(jnp.int32, (tile, 1), 0) < rows_ref[0]
            right_in[part, columns] = jnp.where(live, right_in[part, columns] - moved, 0.0)

    gram_step()
    pl.semaphore_wait(barrier, len(partners))
    g_copy = send(g_ref, g_got, 0)
    column_step(right_loads, right_in, s_ref, store_right)
    s_copies = [send(s_ref.at[:, give], s_got[0], 0)]
    g_copy.wait_recv()
    pairs, small = 2 * rank, rank // 2
    sum_one[...] = g_ref[rank:, :] + g_got[rank:, :]
    one_cross = send(sum_one.at[:rank, pairs:], got_tail.at[:rank], 1)
    part = pl.ds(pl.multiple_of(rank + mine * small, 8), small)
    area = pl.ds(pl.multiple_of(mine * small, 8), small)
    near_copies = [
        send(sum_one.at[part, pairs:], near.at[0, area], 2),
        send(sum_one.at[part, pairs:], near.at[1, area], 1, 2),
    ]
    tail = pl.ds(pl.multiple_of(rank + mine * rank, 8), rank)
    one_tail = send(sum_one.at[tail, pairs:], got_tail.at[tail], 1)
    prepare(0, g_ref[:rank, :], g_got[:rank, :], slice(rank, None))
    solve(0, rows - rank)
    column_step(cot_loads, cot_in, k_ref, store_cot)
    k_copy = send(k_ref.at[:, give], k_got[0], 0)
    l_own[...] = s_ref[:rank, keep] - turned(g_ref[:rank, :pairs], z_own[0])[:rank]
    l_zero = s_got[0][:rank, :] - turned(g_got[:rank, :pairs], z_sib[0])[:rank]
    k_copy.wait_recv()
    k_sum[1][...] = k_ref[rank:, keep] + k_got[0][rank:, :]
    k_last_one = send(k_sum[1].at[pairs:], k_got[1].at[pairs:], 1)
    k_one = send(k_sum[1].at[:pairs], k_got[1].at[:pairs], 1)
    head = share((rows - rank) // 2)
    one_head = send(sum_one.at[head, :pairs], got_head.at[head], 1)
    one_cross.wait_recv()
    prepare(1, sum_one[:rank, pairs:], got_tail[:rank], slice(None))
    one_tail.wait_recv()
    tail_relay = relay(got_tail.at[tail])
    for copy in near_copies:
        copy.wait_recv()
    near_relay = relay(near.at[:, area])
    tail_relay.wait_recv()
    sum_two[...] = sum_one[rank:, pairs:] + got_tail[rank:]
    two_copy = send(sum_two.at[rank:], got_two.at[rank:], 2)
    solve(1, pairs)
    near_relay.wait_recv()
    got_two[:rank] = near[0] + near[1]
    prepare(2, sum_two[:rank], got_two[:rank], slice(rank, None))
    k_last_one.wait_recv()
    k_sum[3][...] = k_sum[1][pairs:] + k_got[1][pairs:]
    far_copies = [send(k_sum[3], far.at[0], 3), send(k_sum[3], far.at[1], 2, 3)]
    k_one.wait_recv()
    k_sum[2][:rank] = k_sum[1][rank:pairs] + k_got[1][rank:pairs]
    k_two = send(k_sum[2].at[:rank], k_got[2].at[:rank], 2)
    two_copy.wait_recv()
    sum_three[...] = sum_two[rank:] + got_two[rank:]
    three_copy = send(sum_three, got_three, 3)
    solve(2, rank)
    z_early = send(z_ship.at[: last * rank], z_out.at[: last * rank, keep], 0)
    one_head.wait_recv()
    head_relay = relay(got_head.at[head])
    row = slice(rank, 2 * rank)
    l_own[...] -= turned(g_ref[row, :pairs], z_own[1])[:rank]
    row = slice(2 * rank, 3 * rank)
    l_own[...] -= turned(g_ref[row, :pairs], z_own[2])[:rank]
    l_two = s_got[2][:rank, :] - turned(got_two[:rank], z_sib[2])[:rank]
    head_relay.wait_recv()
    row = slice(rank, 2 * rank)
    mixed = jnp.concatenate(
        [jnp.where(left_lanes, g_got[row, :pairs], 0.0), jnp.where(left_lanes, 0.0, got_head[:rank])], 0
    )
    change = turned(mixed, jnp.concatenate([z_own[1], z_sib[1]], 0))
    row = slice(2 * rank, 3 * rank)
    mixed = jnp.where(left_lanes, g_got[row, :pairs], got_head[rank : 2 * rank])
    change = change + turned(mixed, z_own[2])
    l_zero = l_zero - change[:rank]
    l_one = s_got[1][:rank, :] - change[rank:]
    z_early.wait_recv()
    move_early()
    three_copy.wait_recv()
    row = slice(3 * rank, 4 * rank)
    nothing = jnp.zeros((rank, pairs), jnp.float32)
    own = jnp.concatenate(
        [
            jnp.where(left_lanes, g_got[row, :pairs], got_head[2 * rank :]),
            jnp.where(left_lanes, got_two[rank:], 0.0),
            g_ref[row, :pairs],
        ],
        1,
    )
    sibling = jnp.concatenate([nothing, jnp.where(left_lanes, 0.0, got_three[...]), nothing], 1)
    prepare(3, own, sibling, slice(0, 5 * rank))
    change = solve(3, 5 * rank)
    z_late = send(z_ship.at[last * rank :], z_out.at[last * rank :, keep], 0)
    final = jnp.concatenate([l_zero, l_one, l_two, s_got[3][...]], 0) - change[: 4 * rank]
    l_out[:, keep] = final * scale
    l_ship[:rank] = (l_own[...] - change[4 * rank :]) * scale
    l_ship[rank:] = final[rank:] * scale
    l_copy = send(l_ship, l_out.at[:, keep], 0)
    for copy in far_copies:
        copy.wait_recv()
    k_two.wait_recv()
    k_sib = [k_got[level][:rank, :] for level in range(last)] + [far[0] + far[1]]
    for level in range(levels):
        value = k_sib[level] * scale
        k_out[block(level), keep] = value
        k_ship[block(level)] = k_ref[:rank, keep] * scale if level == 0 else value
    k_final = send(k_ship, k_out.at[:, keep], 0)
    move_late(keep)
    z_late.wait_recv()
    move_late(give)
    l_copy.wait_recv()
    k_final.wait_recv()
    for copy in sends:
        copy.wait_send()


def tree_steps(
    levels, rank, base, steps, s_ref, k_ref, g_ref, node_ref, z_out, l_out, k_out, scratch
):
    inverse = scratch[0]
    own = [None] + [scratch[1 + 3 * n : 4 + 3 * n] for n in range(levels - 1)]
    start = 1 + 3 * (levels - 1)
    got = [scratch[start + 3 * n : start + 3 * n + 3] for n in range(levels)]
    start += 3 * levels
    packed, other, node_sem, send_sem, recv_sem = scratch[start:]
    cols = s_ref.shape[1]
    half = cols // 2
    position = lax.axis_index("leaf")

    def bit_of(height):
        return lax.rem(lax.div(position, 2 ** (base + height)), 2)

    def partner(height):
        return position + (1 - 2 * bit_of(height)) * 2 ** (base + height)

    fetches = []
    for height in range(levels):
        offset = 2**levels - 2 ** (levels - height)
        node = offset + lax.div(position, 2 ** (base + height + 1))
        fetch = pltpu.make_async_copy(node_ref.at[node], inverse.at[height], node_sem.at[height])
        fetch.start()
        fetches.append(fetch)

    barrier = pltpu.get_barrier_semaphore()
    for height in range(levels):
        pl.semaphore_signal(
            barrier, inc=1, device_id={"leaf": partner(height)}, device_id_type=MESH
        )
    steps[0]()
    pl.semaphore_wait(barrier, levels)

    def send(source, target, height, slot):
        copy = pltpu.make_async_remote_copy(
            src_ref=source,
            dst_ref=target,
            send_sem=send_sem.at[slot],
            recv_sem=recv_sem.at[slot],
            device_id={"leaf": partner(height)},
            device_id_type=MESH,
        )
        copy.start()
        return copy

    mine = bit_of(0)
    keep = pl.ds(pl.multiple_of(mine * half, half), half)
    give = pl.ds(pl.multiple_of((1 - mine) * half, half), half)
    s_all = [s_ref.at[:, keep]] + [own[n][0] for n in range(1, levels)]
    g_all = [g_ref] + [own[n][1] for n in range(1, levels)]
    k_all = [k_ref.at[:, keep]] + [own[n][2] for n in range(1, levels)]
    sends = []

    def half_rows(height):
        size = g_all[height].shape[0] // 2
        return pl.ds(pl.multiple_of(mine * size, 8), size)

    def advance_gram(height, copy):
        copy.wait_recv()
        if 0 < height < levels - 1:
            area = got[height][1].at[half_rows(height), :]
            relay = send(area, area, 0, 3 * levels + 2 + height)
            sends.append(relay)
            relay.wait_recv()
        if height == levels - 1:
            return None
        g_now, g_got, g_next = g_all[height], got[height][1], g_all[height + 1]
        skip = g_now.shape[1] - g_next.shape[1]
        g_next[...] = g_now[rank:, skip:] + g_got[rank:, skip:]
        source, target = g_next, got[height + 1][1]
        if height < levels - 2:
            area = half_rows(height + 1)
            source, target = source.at[area, :], target.at[area, :]
        sends.append(send(source, target, height + 1, 3 * height + 4))
        return sends[-1]

    g_copy = send(g_ref, got[0][1], 0, 1)
    sends.append(g_copy)
    steps[1]()
    s_copy = send(s_ref.at[:, give], got[0][0], 0, 0)
    sends.append(s_copy)
    g_copy = advance_gram(0, g_copy)
    steps[2]()
    k_copy = send(k_ref.at[:, give], got[0][2], 0, 2)
    sends.append(k_copy)
    z_own, z_sib = [], []
    for height in range(levels):
        shift = rank * height - rank * height // 128 * 128
        s_now, g_now, k_now = s_all[height], g_all[height], k_all[height]
        s_got, g_got, k_got = got[height]
        s_copy.wait_recv()
        lower = bit_of(height) == 0
        here, there = s_now[:rank, :], s_got[:rank, :]
        pair = jnp.concatenate(
            [jnp.where(lower, here, there), jnp.where(lower, there, here)], 0
        )
        fetches[height].wait()
        z = dot(inverse[height], pair)
        z_own.append(jnp.where(lower, z[:rank], z[rank:]))
        z_sib.append(jnp.where(lower, z[rank:], z[:rank]))
        if height < levels - 1:
            s_next, _, k_next = own[height + 1]
            block = slice(shift, shift + rank)
            s_next[...] = (
                s_now[rank:, :]
                + s_got[rank:, :]
                - dot(g_now[rank:, :][:, block], z_own[-1])
                - dot(g_got[rank:, :][:, block], z_sib[-1])
            )
            s_copy = send(s_next, got[height + 1][0], height + 1, 3 * height + 3)
            sends.append(s_copy)
            k_copy.wait_recv()
            k_next[...] = k_now[rank:, :] + k_got[rank:, :]
            k_copy = send(k_next, got[height + 1][2], height + 1, 3 * height + 5)
            sends.append(k_copy)
            g_copy = advance_gram(height + 1, g_copy)
    rows = levels * rank
    scale = 1.0 / math.sqrt(cols)
    z_all = jnp.concatenate(z_own, 0)
    areas = [pl.ds(n * rows, rows) for n in range(3)]
    packed[:rank, :] = z_sib[0]
    packed[rank:rows, :] = z_all[rank:]
    last = [send(packed.at[areas[0]], other.at[areas[0]], 0, 3 * levels)]
    z_out[:, keep] = z_all
    l_first = (s_ref[:rank, keep] - dot(g_ref[:rank, :], z_all)) * scale
    packed[rows : rows + rank, :] = l_first
    for height in range(levels):
        shift = rank * height - rank * height // 128 * 128
        part = slice(height * rank, (height + 1) * rank)
        chain = jnp.concatenate([z_sib[height]] + z_own[height + 1 :], 0)
        row = got[height][1][:rank, :][:, shift:]
        l_part = (got[height][0][:rank, :] - dot(row, chain)) * scale
        l_out[part, keep] = l_part
        if height > 0:
            packed[rows + height * rank : rows + (height + 1) * rank, :] = l_part
    last.append(send(packed.at[areas[1]], other.at[areas[1]], 0, 3 * levels + 1))
    k_copy.wait_recv()
    packed[2 * rows : 2 * rows + rank, :] = k_ref[:rank, keep] * scale
    for height in range(levels):
        part = slice(height * rank, (height + 1) * rank)
        k_part = got[height][2][:rank, :] * scale
        k_out[part, keep] = k_part
        if height > 0:
            packed[2 * rows + height * rank : 2 * rows + (height + 1) * rank, :] = k_part
    last.append(send(packed.at[areas[2]], other.at[areas[2]], 0, 3 * levels + 2))
    for copy, target, area in zip(last, (z_out, l_out, k_out), areas):
        copy.wait_recv()
        target[:, give] = other[area, :]
    for copy in sends + last:
        copy.wait_send()


def tree_scratch(levels, rank, rows, cols, node_shape):
    half = cols // 2
    own, got = [], []
    for height in range(levels):
        left = rows - rank * height
        wide = rows - rank * height // 128 * 128
        group = [
            pltpu.VMEM((left, half), jnp.float32),
            pltpu.VMEM((left, wide), jnp.float32),
            pltpu.VMEM((left, half), jnp.float32),
        ]
        got += group
        if height > 0:
            own += group
    count = 4 * levels + 1
    return (
        [pltpu.VMEM((levels,) + node_shape, jnp.float32)]
        + own
        + got
        + [
            pltpu.VMEM((3 * rows, half), jnp.float32),
            pltpu.VMEM((3 * rows, half), jnp.float32),
            pltpu.SemaphoreType.DMA((levels,)),
            pltpu.SemaphoreType.DMA((count,)),
            pltpu.SemaphoreType.DMA((count,)),
        ]
    )


def tree(sums, weight_sums, gram, node_inverse, levels, rank, base):
    rows, cols = sums.shape
    vmem = pl.BlockSpec(memory_space=pltpu.VMEM)
    return pl.pallas_call(
        functools.partial(tree_kernel, levels, rank, base),
        out_shape=[jax.ShapeDtypeStruct((rows, cols), jnp.float32)] * 3,
        in_specs=[vmem] * 3 + [pl.BlockSpec(memory_space=pl.ANY)],
        out_specs=[vmem] * 3,
        scratch_shapes=tree_scratch(levels, rank, rows, cols, node_inverse.shape[1:]),
        compiler_params=pltpu.CompilerParams(collective_id=0, has_side_effects=True),
    )(sums, weight_sums, gram, node_inverse)


def whole_tree(leaf_rows, right_side, cotangent, basis, saved, node_inverse, levels, rank, tile):
    rows, depth = basis.shape
    cols = right_side.shape[1]
    vmem = pl.BlockSpec(memory_space=pltpu.VMEM)
    hbm = pl.BlockSpec(memory_space=pltpu.HBM)
    args = (right_side, cotangent, basis, saved, node_inverse)
    shapes = (
        [((rows, cols), jnp.float32)] * 2
        + [((depth, cols), jnp.float32)]
        + [((depth, cols), jnp.bfloat16)] * 2
    )
    return pl.pallas_call(
        functools.partial(whole_kernel, levels, rank, tile),
        out_shape=[pltpu.VMEM(shape, dtype) for shape, dtype in shapes],
        in_specs=[pl.BlockSpec(memory_space=pltpu.SMEM)] + [hbm] * 5,
        out_specs=[vmem] * 5,
        scratch_shapes=whole_scratch(levels, rank, rows, cols, depth, depth // tile),
        compiler_params=pltpu.CompilerParams(
            collective_id=0, has_side_effects=True, vmem_limit_bytes=VMEM_TREE
        ),
    )(leaf_rows, *[pltpu.with_memory_space_constraint(arg, pltpu.HBM) for arg in args])


def whole_scratch(levels, rank, rows, cols, depth, tiles):
    half, pairs = cols // 2, 2 * rank

    def full(*shape):
        return pltpu.VMEM(shape, jnp.float32)

    def short(*shape):
        return pltpu.VMEM(shape, jnp.bfloat16)

    steps = [full(rows - rank * height, half) for height in range(levels)]
    return (
        [full(rows, cols), short(rows, depth), short(rows, depth)]
        + [full(rows, cols), full(rows, cols), full(rows, rows), full(rows, rows)]
        + [full(depth, cols)]
        + [full(rows, depth)] * 2
        + [short(rows, depth)] * 2
        + [full(levels, pairs, pairs)]
        + [short(pairs + rows + pairs, pairs)] * 2
        + [full(rank, half)]
        + [full(rows, half)] * 3
        + [
            pltpu.SemaphoreType.DMA((4, tiles)),
            pltpu.SemaphoreType.DMA((levels,)),
            pltpu.SemaphoreType.DMA((SLOTS,)),
            pltpu.SemaphoreType.DMA((SLOTS,)),
        ]
        + steps * 4
        + [
            full(rows - rank, rows),
            full(rows - rank, pairs),
            full(rows - rank, pairs),
            full(pairs, pairs),
            full(pairs, pairs),
            full(rank, pairs),
            full(rank, pairs),
            full(2, rank, pairs),
            full(2, rank, half),
        ]
    )


def finish_kernel(
    tile,
    rows_ref,
    l_ref,
    k_ref,
    x_ref,
    cot_high,
    cot_low,
    x_hbm,
    left_hbm,
    grad_hbm,
    left_ref,
    grad_ref,
    sem,
):
    tiles = x_ref.shape[0] // tile
    copies = []

    def out(source, target, index, kind, n):
        copy = pltpu.make_async_copy(source.at[index], target.at[index], sem.at[kind, n])
        copy.start()
        copies.append(copy)

    left, right = split(l_ref[...]), split(k_ref[...])
    for n in range(tiles):
        out(x_ref, x_hbm, (slice(n * tile, (n + 1) * tile), slice(None)), 0, n)
    for n in range(tiles):
        part = slice(n * tile, (n + 1) * tile)
        down, across = (part, slice(None)), (slice(None), part)
        value = triple(left, (cot_high[down], cot_low[down]), ((1,), (1,)))
        live = n * tile + lax.broadcasted_iota(jnp.int32, (1, tile), 1) < rows_ref[0]
        left_ref[across] = jnp.where(live, value, 0.0).astype(jnp.bfloat16)
        out(left_ref, left_hbm, across, 1, n)
        value = triple(right, split(x_ref[down]), ((1,), (1,)))
        grad_ref[across] = value.astype(jnp.bfloat16)
        out(grad_ref, grad_hbm, across, 2, n)
    for copy in copies:
        copy.wait()


def finish(leaf_rows, parts, tile):
    depth, cols = parts[2].shape
    rows = parts[0].shape[0]
    vmem = pl.BlockSpec(memory_space=pltpu.VMEM)
    hbm = pl.BlockSpec(memory_space=pltpu.HBM)
    shapes = [
        ((depth, cols), jnp.float32),
        ((rows, depth), jnp.bfloat16),
        ((rows, depth), jnp.bfloat16),
    ]
    return pl.pallas_call(
        functools.partial(finish_kernel, tile),
        out_shape=[pltpu.HBM(shape, dtype) for shape, dtype in shapes],
        in_specs=[pl.BlockSpec(memory_space=pltpu.SMEM)] + [vmem] * 5,
        out_specs=[hbm] * 3,
        scratch_shapes=[pltpu.VMEM(shape, dtype) for shape, dtype in shapes[1:]]
        + [pltpu.SemaphoreType.DMA((3, depth // tile))],
        compiler_params=pltpu.CompilerParams(vmem_limit_bytes=VMEM_FINISH),
    )(leaf_rows, *[pltpu.with_memory_space_constraint(part, pltpu.VMEM) for part in parts])


def split(value):
    high = value.astype(jnp.bfloat16)
    return high, (value - high.astype(jnp.float32)).astype(jnp.bfloat16)


def triple(left, right, dims):
    def one(a, b):
        return lax.dot_general(a, b, (dims, ((), ())), preferred_element_type=jnp.float32)

    return one(left[0], right[1]) + one(left[1], right[0]) + one(left[0], right[0])


def lead_kernel(rows_ref, right_ref, cot_ref, basis_ref, saved_ref, s_ref, k_ref, g_ref):
    step = pl.program_id(0)
    tile = basis_ref.shape[1]
    place = step * tile + lax.broadcasted_iota(jnp.int32, (1, tile), 1)
    basis = split(jnp.where(place < rows_ref[0], basis_ref[...], 0.0))
    s_now = triple(basis, split(right_ref[...]), ((1,), (0,)))
    k_now = triple(basis, split(cot_ref[...]), ((1,), (0,)))
    g_now = triple(basis, split(saved_ref[...]), ((1,), (1,)))

    @pl.when(step == 0)
    def _():
        s_ref[...] = s_now
        k_ref[...] = k_now
        g_ref[...] = g_now

    @pl.when(step > 0)
    def _():
        s_ref[...] += s_now
        k_ref[...] += k_now
        g_ref[...] += g_now


def close_kernel(
    rows_ref, right_ref, cot_ref, saved_ref, z_ref, l_ref, k_ref, x_ref, left_ref, grad_ref
):
    tile = saved_ref.shape[1]
    first = pl.program_id(0) * tile
    down = first + lax.broadcasted_iota(jnp.int32, (tile, 1), 0)
    across = first + lax.broadcasted_iota(jnp.int32, (1, tile), 1)
    moved = triple(split(saved_ref[...]), split(z_ref[...]), ((0,), (0,)))
    solved = jnp.where(down < rows_ref[0], right_ref[...] - moved, 0.0)
    x_ref[...] = solved
    left = triple(split(l_ref[...]), split(cot_ref[...]), ((1,), (1,)))
    left_ref[...] = jnp.where(across < rows_ref[0], left, 0.0).astype(jnp.bfloat16)
    grad = triple(split(k_ref[...]), split(solved), ((1,), (1,)))
    grad_ref[...] = grad.astype(jnp.bfloat16)


def body(right_side, cotangent, coeff_basis, saved_basis, node_inverse, leaf_rows):
    row_count, cols = right_side.shape
    levels, rank = coeff_basis.shape[0], coeff_basis.shape[1]
    height = levels * rank
    base = lax.axis_size("leaf").bit_length() - 1 - levels
    basis = coeff_basis.reshape(height, row_count)
    saved = saved_basis.reshape(height, row_count)
    tile = math.gcd(row_count, TILE)
    grid = (row_count // tile,)
    count = pl.BlockSpec(memory_space=pltpu.SMEM)
    tall = pl.BlockSpec((tile, cols), lambda i: (i, 0))
    wide = pl.BlockSpec((height, tile), lambda i: (0, i))
    small = pl.BlockSpec((height, cols), lambda i: (0, 0))
    square = pl.BlockSpec((height, height), lambda i: (0, 0))
    if base == 0:
        parts = whole_tree(
            leaf_rows, right_side, cotangent, basis, saved, node_inverse, levels, rank, tile
        )
        current, left, right = finish(leaf_rows, parts, tile)
    else:
        sums, weight_sums, gram = pl.pallas_call(
            lead_kernel,
            grid=grid,
            out_shape=[
                jax.ShapeDtypeStruct((height, cols), jnp.float32),
                jax.ShapeDtypeStruct((height, cols), jnp.float32),
                jax.ShapeDtypeStruct((height, height), jnp.float32),
            ],
            in_specs=[count, tall, tall, wide, wide],
            out_specs=[small, small, square],
        )(leaf_rows, right_side, cotangent, basis, saved)
        for bit in range(base):
            sums = sums + swapped(sums, bit)
            weight_sums = weight_sums + swapped(weight_sums, bit)
            gram = gram + swapped(gram, bit)
        z_own, l_sib, k_sib = tree(sums, weight_sums, gram, node_inverse, levels, rank, base)
        current, left, right = pl.pallas_call(
            close_kernel,
            grid=grid,
            out_shape=[
                jax.ShapeDtypeStruct((row_count, cols), jnp.float32),
                jax.ShapeDtypeStruct((height, row_count), jnp.bfloat16),
                jax.ShapeDtypeStruct((height, row_count), jnp.bfloat16),
            ],
            in_specs=[count, tall, tall, wide, small, small, small],
            out_specs=[tall, wide, wide],
        )(leaf_rows, right_side, cotangent, saved, z_own, l_sib, k_sib)
    shape = (levels, rank, row_count)
    return current, left.reshape(shape), right.reshape(shape)


def solution(mesh):
    in_specs = (
        P(("groups", "leaf"), None),
        P(("groups", "leaf"), None),
        P(None, None, ("groups", "leaf")),
        P(None, None, ("groups", "leaf")),
        P("groups", None, None),
        P(("groups", "leaf")),
    )
    out_specs = (
        P(("groups", "leaf"), None),
        P(None, None, ("groups", "leaf")),
        P(None, None, ("groups", "leaf")),
    )
    return jax.shard_map(body, mesh=mesh, in_specs=in_specs, out_specs=out_specs, check_vma=False)
```

```python
import functools
import math

import jax
import jax.numpy as jnp
from jax import lax
from jax.experimental import pallas as pl
from jax.experimental.pallas import tpu as pltpu
from jax.sharding import PartitionSpec as P

MESH = pl.DeviceIdType.MESH
TILE = 512
SLOTS = 32
VMEM_TREE = 32 * 2**20
VMEM_FINISH = 16 * 2**20


def swapped(value, bit):
    mask = 2**bit
    pairs = [(source, source ^ mask) for source in range(lax.axis_size("leaf"))]
    return lax.ppermute(value, "leaf", pairs)


def dot(a, b, dims=((1,), (0,))):
    return triple(split(a), split(b), dims)


def tree_kernel(
    levels, rank, base, s_ref, k_ref, g_ref, node_ref, z_out, l_out, k_out, *scratch
):
    steps = [lambda: None] * 3
    tree_steps(
        levels, rank, base, steps, s_ref, k_ref, g_ref, node_ref, z_out, l_out, k_out, scratch
    )


def whole_kernel(
    levels,
    rank,
    tile,
    rows_ref,
    right_ref,
    cot_ref,
    basis_ref,
    saved_ref,
    node_ref,
    l_out,
    k_out,
    right_in,
    cot_high,
    cot_low,
    z_out,
    saved_high,
    saved_low,
    s_ref,
    k_ref,
    g_ref,
    g_got,
    cot_in,
    basis_in,
    saved_in,
    high_ref,
    low_ref,
    inverse,
    mix_high,
    mix_low,
    l_own,
    l_ship,
    k_ship,
    z_ship,
    load_sem,
    node_sem,
    send_sem,
    recv_sem,
    *scratch,
):
    depth = basis_ref.shape[1]
    rows, cols = s_ref.shape
    half = cols // 2
    last = levels - 1
    tiles = depth // tile
    scale = 1.0 / math.sqrt(cols)
    position = lax.axis_index("leaf")
    s_got, s_sum, k_got, k_sum = [list(scratch[levels * n : levels * (n + 1)]) for n in range(4)]
    sum_one, got_tail, got_head, sum_two, got_two, sum_three, got_three, near, far = scratch[4 * levels :]

    def bit_of(height):
        return lax.rem(lax.div(position, 2**height), 2)

    def partner(*heights):
        return position + sum((1 - 2 * bit_of(height)) * 2**height for height in heights)

    def block(level, base=0):
        return slice((level - base) * rank, (level - base + 1) * rank)

    def load(source, target, kind, axis):
        copies = []
        for n in range(tiles):
            part = pl.ds(n * tile, tile)
            index = (part, slice(None)) if axis == 0 else (slice(None), part)
            copies.append(
                pltpu.make_async_copy(source.at[index], target.at[index], load_sem.at[kind, n])
            )
        return copies

    basis_loads = load(basis_ref, basis_in, 0, 1)
    saved_loads = load(saved_ref, saved_in, 1, 1)
    right_loads = load(right_ref, right_in, 2, 0)
    cot_loads = load(cot_ref, cot_in, 3, 0)
    for loads in zip(basis_loads, saved_loads, right_loads):
        for one_load in loads:
            one_load.start()
    for one_load in cot_loads:
        one_load.start()
    fetches = []
    for height in range(levels):
        offset = 2**levels - 2 ** (levels - height)
        node = offset + lax.div(position, 2 ** (height + 1))
        fetch = pltpu.make_async_copy(node_ref.at[node], inverse.at[height], node_sem.at[height])
        fetch.start()
        fetches.append(fetch)

    barrier = pltpu.get_barrier_semaphore()
    partners = [(height,) for height in range(levels)] + [(1, 2), (2, 3)]
    for heights in partners:
        pl.semaphore_signal(
            barrier, inc=1, device_id={"leaf": partner(*heights)}, device_id_type=MESH
        )

    sends = []

    def send(source, target, *heights):
        slot = len(sends)
        copy = pltpu.make_async_remote_copy(
            src_ref=source,
            dst_ref=target,
            send_sem=send_sem.at[slot],
            recv_sem=recv_sem.at[slot],
            device_id={"leaf": partner(*heights)},
            device_id_type=MESH,
        )
        copy.start()
        sends.append(copy)
        return copy

    mine = bit_of(0)
    keep = pl.ds(pl.multiple_of(mine * half, half), half)
    give = pl.ds(pl.multiple_of((1 - mine) * half, half), half)

    def gram_step():
        total, sums = None, None
        for n in range(tiles):
            part = slice(n * tile, (n + 1) * tile)
            live = n * tile + lax.broadcasted_iota(jnp.int32, (1, tile), 1) < rows_ref[0]
            basis_loads[n].wait()
            saved_loads[n].wait()
            right_loads[n].wait()
            basis = split(jnp.where(live, basis_in[:, part], 0.0))
            high_ref[:, part], low_ref[:, part] = basis
            saved = split(saved_in[:, part])
            saved_high[:, part], saved_low[:, part] = saved
            term = triple(saved, basis, ((1,), (1,)))
            total = term if total is None else total + term
            term = triple(basis, split(right_in[part, :]), ((1,), (0,)))
            sums = term if sums is None else sums + term
        g_ref[...] = total
        s_ref[...] = sums

    def column_step(loads, source, target, store):
        for one_load in loads:
            one_load.wait()
        total = None
        for n in range(tiles):
            part = slice(n * tile, (n + 1) * tile)
            pair = split(source[part, :])
            store(part, pair)
            term = triple((high_ref[:, part], low_ref[:, part]), pair, ((1,), (0,)))
            total = term if total is None else total + term
        target[...] = total

    def store_right(part, pair):
        pass

    def store_cot(part, pair):
        cot_high[part, :], cot_low[part, :] = pair

    lane = lax.broadcasted_iota(jnp.int32, (1, 2 * rank), 1)
    left_lanes = lane < rank

    def order(height, own, sibling):
        lower = bit_of(height) == 0
        return jnp.concatenate(
            [jnp.where(lower, own, sibling), jnp.where(lower, sibling, own)], 0
        )

    def prepare(height, own, sibling, part):
        fetches[height].wait()
        node = inverse[height]
        cross = dot(order(height, own, sibling), node, ((0,), (0,)))[part]
        high, low = split(jnp.concatenate([node, cross], 0))
        mix_high[: high.shape[0]] = high
        mix_low[: low.shape[0]] = low

    z_own, z_sib = [], []

    def solve(height, count):
        own = s_ref[:, keep] if height == 0 else s_sum[height][...]
        s_copies[0].wait_recv()
        pair = order(height, own[:rank], s_got[height][:rank, :])
        high, low = split(pair)
        size = 2 * rank + count
        wide = one(mix_high[:size], jnp.concatenate([high, low], 1))
        out = wide[:, :half] + wide[:, half:] + one(mix_low[:size], high)
        lower = bit_of(height) == 0
        z_own.append(jnp.where(lower, out[:rank], out[rank : 2 * rank]))
        z_sib.append(jnp.where(lower, out[rank : 2 * rank], out[:rank]))
        change = out[2 * rank :]
        if height < last:
            for copy in s_copies[1:]:
                copy.wait_recv()
            following = own[rank:] + s_got[height][rank:, :] - change
            s_sum[height + 1][...] = following
            target = s_got[height + 1]
            source = s_sum[height + 1]
            s_copies[:] = [send(source.at[:rank], target.at[:rank], height + 1)]
            if height + 1 < last:
                s_copies.append(send(source.at[rank:], target.at[rank:], height + 1))
        z_out[block(height), keep] = z_own[-1]
        z_ship[block(height)] = z_sib[-1] if height == 0 else z_own[-1]
        return change

    def one(a, b):
        return lax.dot_general(
            a, b, (((1,), (0,)), ((), ())), preferred_element_type=jnp.float32
        )

    def turned(a, b):
        return dot(a, b, ((0,), (0,)))

    def share(size):
        return pl.ds(pl.multiple_of(mine * size, 8), size)

    def relay(area):
        return send(area, area, 0)

    def move_early():
        z = split(z_out[: last * rank, :])
        for n in range(tiles):
            part = slice(n * tile, (n + 1) * tile)
            saved = (saved_high[: last * rank, part], saved_low[: last * rank, part])
            right_in[part, :] -= triple(saved, z, ((0,), (0,)))

    def move_late(columns):
        high, low = split(z_out[last * rank :, columns])
        stacked = jnp.concatenate([high, high, low], 0)
        for n in range(tiles):
            part = slice(n * tile, (n + 1) * tile)
            saved = saved_high[last * rank :, part]
            saved = jnp.concatenate([saved, saved_low[last * rank :, part], saved], 0)
            moved = lax.dot_general(
                saved, stacked, (((0,), (0,)), ((), ())), preferred_element_type=jnp.float32
            )
            live = n * tile + lax.broadcasted_iota(jnp.int32, (tile, 1), 0) < rows_ref[0]
            right_in[part, columns] = jnp.where(live, right_in[part, columns] - moved, 0.0)

    gram_step()
    pl.semaphore_wait(barrier, len(partners))
    g_copy = send(g_ref, g_got, 0)
    s_copies = [send(s_ref.at[:, give], s_got[0], 0)]
    g_copy.wait_recv()
    pairs, small = 2 * rank, rank // 2
    sum_one[...] = g_ref[rank:, :] + g_got[rank:, :]
    one_cross = send(sum_one.at[:rank, pairs:], got_tail.at[:rank], 1)
    part = pl.ds(pl.multiple_of(rank + mine * small, 8), small)
    area = pl.ds(pl.multiple_of(mine * small, 8), small)
    near_copies = [
        send(sum_one.at[part, pairs:], near.at[0, area], 2),
        send(sum_one.at[part, pairs:], near.at[1, area], 1, 2),
    ]
    tail = pl.ds(pl.multiple_of(rank + mine * rank, 8), rank)
    one_tail = send(sum_one.at[tail, pairs:], got_tail.at[tail], 1)
    prepare(0, g_ref[:rank, :], g_got[:rank, :], slice(rank, None))
    solve(0, rows - rank)
    column_step(cot_loads, cot_in, k_ref, store_cot)
    k_copy = send(k_ref.at[:, give], k_got[0], 0)
    l_own[...] = s_ref[:rank, keep] - turned(g_ref[:rank, :pairs], z_own[0])[:rank]
    l_zero = s_got[0][:rank, :] - turned(g_got[:rank, :pairs], z_sib[0])[:rank]
    k_copy.wait_recv()
    k_sum[1][...] = k_ref[rank:, keep] + k_got[0][rank:, :]
    k_last_one = send(k_sum[1].at[pairs:], k_got[1].at[pairs:], 1)
    k_one = send(k_sum[1].at[:pairs], k_got[1].at[:pairs], 1)
    head = share((rows - rank) // 2)
    one_head = send(sum_one.at[head, :pairs], got_head.at[head], 1)
    one_cross.wait_recv()
    prepare(1, sum_one[:rank, pairs:], got_tail[:rank], slice(None))
    one_tail.wait_recv()
    tail_relay = relay(got_tail.at[tail])
    for copy in near_copies:
        copy.wait_recv()
    near_relay = relay(near.at[:, area])
    tail_relay.wait_recv()
    sum_two[...] = sum_one[rank:, pairs:] + got_tail[rank:]
    two_copy = send(sum_two.at[rank:], got_two.at[rank:], 2)
    solve(1, pairs)
    near_relay.wait_recv()
    got_two[:rank] = near[0] + near[1]
    prepare(2, sum_two[:rank], got_two[:rank], slice(rank, None))
    k_last_one.wait_recv()
    k_sum[3][...] = k_sum[1][pairs:] + k_got[1][pairs:]
    far_copies = [send(k_sum[3], far.at[0], 3), send(k_sum[3], far.at[1], 2, 3)]
    k_one.wait_recv()
    k_sum[2][:rank] = k_sum[1][rank:pairs] + k_got[1][rank:pairs]
    k_two = send(k_sum[2].at[:rank], k_got[2].at[:rank], 2)
    two_copy.wait_recv()
    sum_three[...] = sum_two[rank:] + got_two[rank:]
    three_copy = send(sum_three, got_three, 3)
    solve(2, rank)
    z_early = send(z_ship.at[: last * rank], z_out.at[: last * rank, keep], 0)
    one_head.wait_recv()
    head_relay = relay(got_head.at[head])
    row = slice(rank, 2 * rank)
    l_own[...] -= turned(g_ref[row, :pairs], z_own[1])[:rank]
    row = slice(2 * rank, 3 * rank)
    l_own[...] -= turned(g_ref[row, :pairs], z_own[2])[:rank]
    l_two = s_got[2][:rank, :] - turned(got_two[:rank], z_sib[2])[:rank]
    head_relay.wait_recv()
    row = slice(rank, 2 * rank)
    mixed = jnp.concatenate(
        [jnp.where(left_lanes, g_got[row, :pairs], 0.0), jnp.where(left_lanes, 0.0, got_head[:rank])], 0
    )
    change = turned(mixed, jnp.concatenate([z_own[1], z_sib[1]], 0))
    row = slice(2 * rank, 3 * rank)
    mixed = jnp.where(left_lanes, g_got[row, :pairs], got_head[rank : 2 * rank])
    change = change + turned(mixed, z_own[2])
    l_zero = l_zero - change[:rank]
    l_one = s_got[1][:rank, :] - change[rank:]
    z_early.wait_recv()
    move_early()
    three_copy.wait_recv()
    row = slice(3 * rank, 4 * rank)
    nothing = jnp.zeros((rank, pairs), jnp.float32)
    own = jnp.concatenate(
        [
            jnp.where(left_lanes, g_got[row, :pairs], got_head[2 * rank :]),
            jnp.where(left_lanes, got_two[rank:], 0.0),
            g_ref[row, :pairs],
        ],
        1,
    )
    sibling = jnp.concatenate([nothing, jnp.where(left_lanes, 0.0, got_three[...]), nothing], 1)
    prepare(3, own, sibling, slice(0, 5 * rank))
    change = solve(3, 5 * rank)
    z_late = send(z_ship.at[last * rank :], z_out.at[last * rank :, keep], 0)
    final = jnp.concatenate([l_zero, l_one, l_two, s_got[3][...]], 0) - change[: 4 * rank]
    l_out[:, keep] = final * scale
    l_ship[:rank] = (l_own[...] - change[4 * rank :]) * scale
    l_ship[rank:] = final[rank:] * scale
    l_copy = send(l_ship, l_out.at[:, keep], 0)
    for copy in far_copies:
        copy.wait_recv()
    k_two.wait_recv()
    k_sib = [k_got[level][:rank, :] for level in range(last)] + [far[0] + far[1]]
    for level in range(levels):
        value = k_sib[level] * scale
        k_out[block(level), keep] = value
        k_ship[block(level)] = k_ref[:rank, keep] * scale if level == 0 else value
    k_final = send(k_ship, k_out.at[:, keep], 0)
    move_late(keep)
    z_late.wait_recv()
    move_late(give)
    l_copy.wait_recv()
    k_final.wait_recv()
    for copy in sends:
        copy.wait_send()


def tree_steps(
    levels, rank, base, steps, s_ref, k_ref, g_ref, node_ref, z_out, l_out, k_out, scratch
):
    inverse = scratch[0]
    own = [None] + [scratch[1 + 3 * n : 4 + 3 * n] for n in range(levels - 1)]
    start = 1 + 3 * (levels - 1)
    got = [scratch[start + 3 * n : start + 3 * n + 3] for n in range(levels)]
    start += 3 * levels
    packed, other, node_sem, send_sem, recv_sem = scratch[start:]
    cols = s_ref.shape[1]
    half = cols // 2
    position = lax.axis_index("leaf")

    def bit_of(height):
        return lax.rem(lax.div(position, 2 ** (base + height)), 2)

    def partner(height):
        return position + (1 - 2 * bit_of(height)) * 2 ** (base + height)

    fetches = []
    for height in range(levels):
        offset = 2**levels - 2 ** (levels - height)
        node = offset + lax.div(position, 2 ** (base + height + 1))
        fetch = pltpu.make_async_copy(node_ref.at[node], inverse.at[height], node_sem.at[height])
        fetch.start()
        fetches.append(fetch)

    barrier = pltpu.get_barrier_semaphore()
    for height in range(levels):
        pl.semaphore_signal(
            barrier, inc=1, device_id={"leaf": partner(height)}, device_id_type=MESH
        )
    steps[0]()
    pl.semaphore_wait(barrier, levels)

    def send(source, target, height, slot):
        copy = pltpu.make_async_remote_copy(
            src_ref=source,
            dst_ref=target,
            send_sem=send_sem.at[slot],
            recv_sem=recv_sem.at[slot],
            device_id={"leaf": partner(height)},
            device_id_type=MESH,
        )
        copy.start()
        return copy

    mine = bit_of(0)
    keep = pl.ds(pl.multiple_of(mine * half, half), half)
    give = pl.ds(pl.multiple_of((1 - mine) * half, half), half)
    s_all = [s_ref.at[:, keep]] + [own[n][0] for n in range(1, levels)]
    g_all = [g_ref] + [own[n][1] for n in range(1, levels)]
    k_all = [k_ref.at[:, keep]] + [own[n][2] for n in range(1, levels)]
    sends = []

    def half_rows(height):
        size = g_all[height].shape[0] // 2
        return pl.ds(pl.multiple_of(mine * size, 8), size)

    def advance_gram(height, copy):
        copy.wait_recv()
        if 0 < height < levels - 1:
            area = got[height][1].at[half_rows(height), :]
            relay = send(area, area, 0, 3 * levels + 2 + height)
            sends.append(relay)
            relay.wait_recv()
        if height == levels - 1:
            return None
        g_now, g_got, g_next = g_all[height], got[height][1], g_all[height + 1]
        skip = g_now.shape[1] - g_next.shape[1]
        g_next[...] = g_now[rank:, skip:] + g_got[rank:, skip:]
        source, target = g_next, got[height + 1][1]
        if height < levels - 2:
            area = half_rows(height + 1)
            source, target = source.at[area, :], target.at[area, :]
        sends.append(send(source, target, height + 1, 3 * height + 4))
        return sends[-1]

    g_copy = send(g_ref, got[0][1], 0, 1)
    sends.append(g_copy)
    steps[1]()
    s_copy = send(s_ref.at[:, give], got[0][0], 0, 0)
    sends.append(s_copy)
    g_copy = advance_gram(0, g_copy)
    steps[2]()
    k_copy = send(k_ref.at[:, give], got[0][2], 0, 2)
    sends.append(k_copy)
    z_own, z_sib = [], []
    for height in range(levels):
        shift = rank * height - rank * height // 128 * 128
        s_now, g_now, k_now = s_all[height], g_all[height], k_all[height]
        s_got, g_got, k_got = got[height]
        s_copy.wait_recv()
        lower = bit_of(height) == 0
        here, there = s_now[:rank, :], s_got[:rank, :]
        pair = jnp.concatenate(
            [jnp.where(lower, here, there), jnp.where(lower, there, here)], 0
        )
        fetches[height].wait()
        z = dot(inverse[height], pair)
        z_own.append(jnp.where(lower, z[:rank], z[rank:]))
        z_sib.append(jnp.where(lower, z[rank:], z[:rank]))
        if height < levels - 1:
            s_next, _, k_next = own[height + 1]
            block = slice(shift, shift + rank)
            s_next[...] = (
                s_now[rank:, :]
                + s_got[rank:, :]
                - dot(g_now[rank:, :][:, block], z_own[-1])
                - dot(g_got[rank:, :][:, block], z_sib[-1])
            )
            s_copy = send(s_next, got[height + 1][0], height + 1, 3 * height + 3)
            sends.append(s_copy)
            k_copy.wait_recv()
            k_next[...] = k_now[rank:, :] + k_got[rank:, :]
            k_copy = send(k_next, got[height + 1][2], height + 1, 3 * height + 5)
            sends.append(k_copy)
            g_copy = advance_gram(height + 1, g_copy)
    rows = levels * rank
    scale = 1.0 / math.sqrt(cols)
    z_all = jnp.concatenate(z_own, 0)
    areas = [pl.ds(n * rows, rows) for n in range(3)]
    packed[:rank, :] = z_sib[0]
    packed[rank:rows, :] = z_all[rank:]
    last = [send(packed.at[areas[0]], other.at[areas[0]], 0, 3 * levels)]
    z_out[:, keep] = z_all
    l_first = (s_ref[:rank, keep] - dot(g_ref[:rank, :], z_all)) * scale
    packed[rows : rows + rank, :] = l_first
    for height in range(levels):
        shift = rank * height - rank * height // 128 * 128
        part = slice(height * rank, (height + 1) * rank)
        chain = jnp.concatenate([z_sib[height]] + z_own[height + 1 :], 0)
        row = got[height][1][:rank, :][:, shift:]
        l_part = (got[height][0][:rank, :] - dot(row, chain)) * scale
        l_out[part, keep] = l_part
        if height > 0:
            packed[rows + height * rank : rows + (height + 1) * rank, :] = l_part
    last.append(send(packed.at[areas[1]], other.at[areas[1]], 0, 3 * levels + 1))
    k_copy.wait_recv()
    packed[2 * rows : 2 * rows + rank, :] = k_ref[:rank, keep] * scale
    for height in range(levels):
        part = slice(height * rank, (height + 1) * rank)
        k_part = got[height][2][:rank, :] * scale
        k_out[part, keep] = k_part
        if height > 0:
            packed[2 * rows + height * rank : 2 * rows + (height + 1) * rank, :] = k_part
    last.append(send(packed.at[areas[2]], other.at[areas[2]], 0, 3 * levels + 2))
    for copy, target, area in zip(last, (z_out, l_out, k_out), areas):
        copy.wait_recv()
        target[:, give] = other[area, :]
    for copy in sends + last:
        copy.wait_send()


def tree_scratch(levels, rank, rows, cols, node_shape):
    half = cols // 2
    own, got = [], []
    for height in range(levels):
        left = rows - rank * height
        wide = rows - rank * height // 128 * 128
        group = [
            pltpu.VMEM((left, half), jnp.float32),
            pltpu.VMEM((left, wide), jnp.float32),
            pltpu.VMEM((left, half), jnp.float32),
        ]
        got += group
        if height > 0:
            own += group
    count = 4 * levels + 1
    return (
        [pltpu.VMEM((levels,) + node_shape, jnp.float32)]
        + own
        + got
        + [
            pltpu.VMEM((3 * rows, half), jnp.float32),
            pltpu.VMEM((3 * rows, half), jnp.float32),
            pltpu.SemaphoreType.DMA((levels,)),
            pltpu.SemaphoreType.DMA((count,)),
            pltpu.SemaphoreType.DMA((count,)),
        ]
    )


def tree(sums, weight_sums, gram, node_inverse, levels, rank, base):
    rows, cols = sums.shape
    vmem = pl.BlockSpec(memory_space=pltpu.VMEM)
    return pl.pallas_call(
        functools.partial(tree_kernel, levels, rank, base),
        out_shape=[jax.ShapeDtypeStruct((rows, cols), jnp.float32)] * 3,
        in_specs=[vmem] * 3 + [pl.BlockSpec(memory_space=pl.ANY)],
        out_specs=[vmem] * 3,
        scratch_shapes=tree_scratch(levels, rank, rows, cols, node_inverse.shape[1:]),
        compiler_params=pltpu.CompilerParams(collective_id=0, has_side_effects=True),
    )(sums, weight_sums, gram, node_inverse)


def whole_tree(leaf_rows, right_side, cotangent, basis, saved, node_inverse, levels, rank, tile):
    rows, depth = basis.shape
    cols = right_side.shape[1]
    vmem = pl.BlockSpec(memory_space=pltpu.VMEM)
    hbm = pl.BlockSpec(memory_space=pltpu.HBM)
    args = (right_side, cotangent, basis, saved, node_inverse)
    shapes = (
        [((rows, cols), jnp.float32)] * 2
        + [((depth, cols), jnp.float32)]
        + [((depth, cols), jnp.bfloat16)] * 2
    )
    return pl.pallas_call(
        functools.partial(whole_kernel, levels, rank, tile),
        out_shape=[pltpu.VMEM(shape, dtype) for shape, dtype in shapes],
        in_specs=[pl.BlockSpec(memory_space=pltpu.SMEM)] + [hbm] * 5,
        out_specs=[vmem] * 5,
        scratch_shapes=whole_scratch(levels, rank, rows, cols, depth, depth // tile),
        compiler_params=pltpu.CompilerParams(
            collective_id=0, has_side_effects=True, vmem_limit_bytes=VMEM_TREE
        ),
    )(leaf_rows, *[pltpu.with_memory_space_constraint(arg, pltpu.HBM) for arg in args])


def whole_scratch(levels, rank, rows, cols, depth, tiles):
    half, pairs = cols // 2, 2 * rank

    def full(*shape):
        return pltpu.VMEM(shape, jnp.float32)

    def short(*shape):
        return pltpu.VMEM(shape, jnp.bfloat16)

    steps = [full(rows - rank * height, half) for height in range(levels)]
    return (
        [full(rows, cols), short(rows, depth), short(rows, depth)]
        + [full(rows, cols), full(rows, cols), full(rows, rows), full(rows, rows)]
        + [full(depth, cols)]
        + [full(rows, depth)] * 2
        + [short(rows, depth)] * 2
        + [full(levels, pairs, pairs)]
        + [short(pairs + rows + pairs, pairs)] * 2
        + [full(rank, half)]
        + [full(rows, half)] * 3
        + [
            pltpu.SemaphoreType.DMA((4, tiles)),
            pltpu.SemaphoreType.DMA((levels,)),
            pltpu.SemaphoreType.DMA((SLOTS,)),
            pltpu.SemaphoreType.DMA((SLOTS,)),
        ]
        + steps * 4
        + [
            full(rows - rank, rows),
            full(rows - rank, pairs),
            full(rows - rank, pairs),
            full(pairs, pairs),
            full(pairs, pairs),
            full(rank, pairs),
            full(rank, pairs),
            full(2, rank, pairs),
            full(2, rank, half),
        ]
    )


def finish_kernel(
    tile,
    rows_ref,
    l_ref,
    k_ref,
    x_ref,
    cot_high,
    cot_low,
    x_hbm,
    left_hbm,
    grad_hbm,
    left_ref,
    grad_ref,
    sem,
):
    tiles = x_ref.shape[0] // tile
    copies = []

    def out(source, target, index, kind, n):
        copy = pltpu.make_async_copy(source.at[index], target.at[index], sem.at[kind, n])
        copy.start()
        copies.append(copy)

    left, right = split(l_ref[...]), split(k_ref[...])
    for n in range(tiles):
        out(x_ref, x_hbm, (slice(n * tile, (n + 1) * tile), slice(None)), 0, n)
    for n in range(tiles):
        part = slice(n * tile, (n + 1) * tile)
        down, across = (part, slice(None)), (slice(None), part)
        value = triple(left, (cot_high[down], cot_low[down]), ((1,), (1,)))
        live = n * tile + lax.broadcasted_iota(jnp.int32, (1, tile), 1) < rows_ref[0]
        left_ref[across] = jnp.where(live, value, 0.0).astype(jnp.bfloat16)
        out(left_ref, left_hbm, across, 1, n)
        value = triple(right, split(x_ref[down]), ((1,), (1,)))
        grad_ref[across] = value.astype(jnp.bfloat16)
        out(grad_ref, grad_hbm, across, 2, n)
    for copy in copies:
        copy.wait()


def finish(leaf_rows, parts, tile):
    depth, cols = parts[2].shape
    rows = parts[0].shape[0]
    vmem = pl.BlockSpec(memory_space=pltpu.VMEM)
    hbm = pl.BlockSpec(memory_space=pltpu.HBM)
    shapes = [
        ((depth, cols), jnp.float32),
        ((rows, depth), jnp.bfloat16),
        ((rows, depth), jnp.bfloat16),
    ]
    return pl.pallas_call(
        functools.partial(finish_kernel, tile),
        out_shape=[pltpu.HBM(shape, dtype) for shape, dtype in shapes],
        in_specs=[pl.BlockSpec(memory_space=pltpu.SMEM)] + [vmem] * 5,
        out_specs=[hbm] * 3,
        scratch_shapes=[pltpu.VMEM(shape, dtype) for shape, dtype in shapes[1:]]
        + [pltpu.SemaphoreType.DMA((3, depth // tile))],
        compiler_params=pltpu.CompilerParams(vmem_limit_bytes=VMEM_FINISH),
    )(leaf_rows, *[pltpu.with_memory_space_constraint(part, pltpu.VMEM) for part in parts])


def split(value):
    high = value.astype(jnp.bfloat16)
    return high, (value - high.astype(jnp.float32)).astype(jnp.bfloat16)


def triple(left, right, dims):
    def one(a, b):
        return lax.dot_general(a, b, (dims, ((), ())), preferred_element_type=jnp.float32)

    return one(left[0], right[1]) + one(left[1], right[0]) + one(left[0], right[0])


def lead_kernel(rows_ref, right_ref, cot_ref, basis_ref, saved_ref, s_ref, k_ref, g_ref):
    step = pl.program_id(0)
    tile = basis_ref.shape[1]
    place = step * tile + lax.broadcasted_iota(jnp.int32, (1, tile), 1)
    basis = split(jnp.where(place < rows_ref[0], basis_ref[...], 0.0))
    s_now = triple(basis, split(right_ref[...]), ((1,), (0,)))
    k_now = triple(basis, split(cot_ref[...]), ((1,), (0,)))
    g_now = triple(basis, split(saved_ref[...]), ((1,), (1,)))

    @pl.when(step == 0)
    def _():
        s_ref[...] = s_now
        k_ref[...] = k_now
        g_ref[...] = g_now

    @pl.when(step > 0)
    def _():
        s_ref[...] += s_now
        k_ref[...] += k_now
        g_ref[...] += g_now


def close_kernel(
    rows_ref, right_ref, cot_ref, saved_ref, z_ref, l_ref, k_ref, x_ref, left_ref, grad_ref
):
    tile = saved_ref.shape[1]
    first = pl.program_id(0) * tile
    down = first + lax.broadcasted_iota(jnp.int32, (tile, 1), 0)
    across = first + lax.broadcasted_iota(jnp.int32, (1, tile), 1)
    moved = triple(split(saved_ref[...]), split(z_ref[...]), ((0,), (0,)))
    solved = jnp.where(down < rows_ref[0], right_ref[...] - moved, 0.0)
    x_ref[...] = solved
    left = triple(split(l_ref[...]), split(cot_ref[...]), ((1,), (1,)))
    left_ref[...] = jnp.where(across < rows_ref[0], left, 0.0).astype(jnp.bfloat16)
    grad = triple(split(k_ref[...]), split(solved), ((1,), (1,)))
    grad_ref[...] = grad.astype(jnp.bfloat16)


def body(right_side, cotangent, coeff_basis, saved_basis, node_inverse, leaf_rows):
    row_count, cols = right_side.shape
    levels, rank = coeff_basis.shape[0], coeff_basis.shape[1]
    height = levels * rank
    base = lax.axis_size("leaf").bit_length() - 1 - levels
    basis = coeff_basis.reshape(height, row_count)
    saved = saved_basis.reshape(height, row_count)
    tile = math.gcd(row_count, TILE)
    grid = (row_count // tile,)
    count = pl.BlockSpec(memory_space=pltpu.SMEM)
    tall = pl.BlockSpec((tile, cols), lambda i: (i, 0))
    wide = pl.BlockSpec((height, tile), lambda i: (0, i))
    small = pl.BlockSpec((height, cols), lambda i: (0, 0))
    square = pl.BlockSpec((height, height), lambda i: (0, 0))
    if base == 0:
        parts = whole_tree(
            leaf_rows, right_side, cotangent, basis, saved, node_inverse, levels, rank, tile
        )
        current, left, right = finish(leaf_rows, parts, tile)
    else:
        sums, weight_sums, gram = pl.pallas_call(
            lead_kernel,
            grid=grid,
            out_shape=[
                jax.ShapeDtypeStruct((height, cols), jnp.float32),
                jax.ShapeDtypeStruct((height, cols), jnp.float32),
                jax.ShapeDtypeStruct((height, height), jnp.float32),
            ],
            in_specs=[count, tall, tall, wide, wide],
            out_specs=[small, small, square],
        )(leaf_rows, right_side, cotangent, basis, saved)
        for bit in range(base):
            sums = sums + swapped(sums, bit)
            weight_sums = weight_sums + swapped(weight_sums, bit)
            gram = gram + swapped(gram, bit)
        z_own, l_sib, k_sib = tree(sums, weight_sums, gram, node_inverse, levels, rank, base)
        current, left, right = pl.pallas_call(
            close_kernel,
            grid=grid,
            out_shape=[
                jax.ShapeDtypeStruct((row_count, cols), jnp.float32),
                jax.ShapeDtypeStruct((height, row_count), jnp.bfloat16),
                jax.ShapeDtypeStruct((height, row_count), jnp.bfloat16),
            ],
            in_specs=[count, tall, tall, wide, small, small, small],
            out_specs=[tall, wide, wide],
        )(leaf_rows, right_side, cotangent, saved, z_own, l_sib, k_sib)
    shape = (levels, rank, row_count)
    return current, left.reshape(shape), right.reshape(shape)


def solution(mesh):
    in_specs = (
        P(("groups", "leaf"), None),
        P(("groups", "leaf"), None),
        P(None, None, ("groups", "leaf")),
        P(None, None, ("groups", "leaf")),
        P("groups", None, None),
        P(("groups", "leaf")),
    )
    out_specs = (
        P(("groups", "leaf"), None),
        P(None, None, ("groups", "leaf")),
        P(None, None, ("groups", "leaf")),
    )
    return jax.shard_map(body, mesh=mesh, in_specs=in_specs, out_specs=out_specs, check_vma=False)
```

```python
import functools
import math

import jax
import jax.numpy as jnp
from jax import lax
from jax.experimental import pallas as pl
from jax.experimental.pallas import tpu as pltpu
from jax.sharding import PartitionSpec as P

MESH = pl.DeviceIdType.MESH
TILE = 512
SLOTS = 32
VMEM_TREE = 32 * 2**20
VMEM_FINISH = 16 * 2**20


def swapped(value, bit):
    mask = 2**bit
    pairs = [(source, source ^ mask) for source in range(lax.axis_size("leaf"))]
    return lax.ppermute(value, "leaf", pairs)


def dot(a, b, dims=((1,), (0,))):
    return triple(split(a), split(b), dims)


def tree_kernel(
    levels, rank, base, s_ref, k_ref, g_ref, node_ref, z_out, l_out, k_out, *scratch
):
    steps = [lambda: None] * 3
    tree_steps(
        levels, rank, base, steps, s_ref, k_ref, g_ref, node_ref, z_out, l_out, k_out, scratch
    )


def whole_kernel(
    levels,
    rank,
    tile,
    rows_ref,
    right_ref,
    cot_ref,
    basis_ref,
    saved_ref,
    node_ref,
    l_out,
    k_out,
    right_in,
    cot_high,
    cot_low,
    z_out,
    saved_high,
    saved_low,
    s_ref,
    k_ref,
    g_ref,
    g_got,
    cot_in,
    basis_in,
    saved_in,
    high_ref,
    low_ref,
    inverse,
    mix_high,
    mix_low,
    l_own,
    l_ship,
    k_ship,
    z_ship,
    load_sem,
    node_sem,
    send_sem,
    recv_sem,
    *scratch,
):
    depth = basis_ref.shape[1]
    rows, cols = s_ref.shape
    half = cols // 2
    last = levels - 1
    tiles = depth // tile
    scale = 1.0 / math.sqrt(cols)
    position = lax.axis_index("leaf")
    s_got, s_sum, k_got, k_sum = [list(scratch[levels * n : levels * (n + 1)]) for n in range(4)]
    sum_one, got_tail, got_head, sum_two, got_two, sum_three, got_three, near, far = scratch[4 * levels :]

    def bit_of(height):
        return lax.rem(lax.div(position, 2**height), 2)

    def partner(*heights):
        return position + sum((1 - 2 * bit_of(height)) * 2**height for height in heights)

    def block(level, base=0):
        return slice((level - base) * rank, (level - base + 1) * rank)

    def load(source, target, kind, axis):
        copies = []
        for n in range(tiles):
            part = pl.ds(n * tile, tile)
            index = (part, slice(None)) if axis == 0 else (slice(None), part)
            copies.append(
                pltpu.make_async_copy(source.at[index], target.at[index], load_sem.at[kind, n])
            )
        return copies

    basis_loads = load(basis_ref, basis_in, 0, 1)
    saved_loads = load(saved_ref, saved_in, 1, 1)
    right_loads = load(right_ref, right_in, 2, 0)
    cot_loads = load(cot_ref, cot_in, 3, 0)
    for loads in zip(basis_loads, saved_loads, right_loads):
        for one_load in loads:
            one_load.start()
    for one_load in cot_loads:
        one_load.start()
    fetches = []
    for height in range(levels):
        offset = 2**levels - 2 ** (levels - height)
        node = offset + lax.div(position, 2 ** (height + 1))
        fetch = pltpu.make_async_copy(node_ref.at[node], inverse.at[height], node_sem.at[height])
        fetch.start()
        fetches.append(fetch)

    barrier = pltpu.get_barrier_semaphore()
    partners = [(height,) for height in range(levels)] + [(1, 2), (2, 3)]
    for heights in partners:
        pl.semaphore_signal(
            barrier, inc=1, device_id={"leaf": partner(*heights)}, device_id_type=MESH
        )

    sends = []

    def send(source, target, *heights):
        slot = len(sends)
        copy = pltpu.make_async_remote_copy(
            src_ref=source,
            dst_ref=target,
            send_sem=send_sem.at[slot],
            recv_sem=recv_sem.at[slot],
            device_id={"leaf": partner(*heights)},
            device_id_type=MESH,
        )
        copy.start()
        sends.append(copy)
        return copy

    mine = bit_of(0)
    keep = pl.ds(pl.multiple_of(mine * half, half), half)
    give = pl.ds(pl.multiple_of((1 - mine) * half, half), half)

    def gram_step():
        total, sums = None, None
        for n in range(tiles):
            part = slice(n * tile, (n + 1) * tile)
            live = n * tile + lax.broadcasted_iota(jnp.int32, (1, tile), 1) < rows_ref[0]
            basis_loads[n].wait()
            saved_loads[n].wait()
            right_loads[n].wait()
            basis = split(jnp.where(live, basis_in[:, part], 0.0))
            high_ref[:, part], low_ref[:, part] = basis
            saved = split(saved_in[:, part])
            saved_high[:, part], saved_low[:, part] = saved
            term = triple(saved, basis, ((1,), (1,)))
            total = term if total is None else total + term
            term = triple(basis, split(right_in[part, :]), ((1,), (0,)))
            sums = term if sums is None else sums + term
        g_ref[...] = total
        s_ref[...] = sums

    def column_step(loads, source, target, store):
        for one_load in loads:
            one_load.wait()
        total = None
        for n in range(tiles):
            part = slice(n * tile, (n + 1) * tile)
            pair = split(source[part, :])
            store(part, pair)
            term = triple((high_ref[:, part], low_ref[:, part]), pair, ((1,), (0,)))
            total = term if total is None else total + term
        target[...] = total

    def store_right(part, pair):
        pass

    def store_cot(part, pair):
        cot_high[part, :], cot_low[part, :] = pair

    lane = lax.broadcasted_iota(jnp.int32, (1, 2 * rank), 1)
    left_lanes = lane < rank

    def order(height, own, sibling):
        lower = bit_of(height) == 0
        return jnp.concatenate(
            [jnp.where(lower, own, sibling), jnp.where(lower, sibling, own)], 0
        )

    def prepare(height, own, sibling, part):
        fetches[height].wait()
        node = inverse[height]
        cross = dot(order(height, own, sibling), node, ((0,), (0,)))[part]
        high, low = split(jnp.concatenate([node, cross], 0))
        mix_high[: high.shape[0]] = high
        mix_low[: low.shape[0]] = low

    z_own, z_sib = [], []

    def solve(height, count):
        own = s_ref[:, keep] if height == 0 else s_sum[height][...]
        s_copies[0].wait_recv()
        pair = order(height, own[:rank], s_got[height][:rank, :])
        high, low = split(pair)
        size = 2 * rank + count
        wide = one(mix_high[:size], jnp.concatenate([high, low], 1))
        out = wide[:, :half] + wide[:, half:] + one(mix_low[:size], high)
        lower = bit_of(height) == 0
        z_own.append(jnp.where(lower, out[:rank], out[rank : 2 * rank]))
        z_sib.append(jnp.where(lower, out[rank : 2 * rank], out[:rank]))
        change = out[2 * rank :]
        if height < last:
            for copy in s_copies[1:]:
                copy.wait_recv()
            following = own[rank:] + s_got[height][rank:, :] - change
            s_sum[height + 1][...] = following
            target = s_got[height + 1]
            source = s_sum[height + 1]
            s_copies[:] = [send(source, target, height + 1)]
        z_out[block(height), keep] = z_own[-1]
        z_ship[block(height)] = z_sib[-1] if height == 0 else z_own[-1]
        return change

    def one(a, b):
        return lax.dot_general(
            a, b, (((1,), (0,)), ((), ())), preferred_element_type=jnp.float32
        )

    def turned(a, b):
        return dot(a, b, ((0,), (0,)))

    def share(size):
        return pl.ds(pl.multiple_of(mine * size, 8), size)

    def relay(area):
        return send(area, area, 0)

    def move_early():
        z = split(z_out[: last * rank, :])
        for n in range(tiles):
            part = slice(n * tile, (n + 1) * tile)
            saved = (saved_high[: last * rank, part], saved_low[: last * rank, part])
            right_in[part, :] -= triple(saved, z, ((0,), (0,)))

    def move_late(columns):
        high, low = split(z_out[last * rank :, columns])
        stacked = jnp.concatenate([high, high, low], 0)
        for n in range(tiles):
            part = slice(n * tile, (n + 1) * tile)
            saved = saved_high[last * rank :, part]
            saved = jnp.concatenate([saved, saved_low[last * rank :, part], saved], 0)
            moved = lax.dot_general(
                saved, stacked, (((0,), (0,)), ((), ())), preferred_element_type=jnp.float32
            )
            live = n * tile + lax.broadcasted_iota(jnp.int32, (tile, 1), 0) < rows_ref[0]
            right_in[part, columns] = jnp.where(live, right_in[part, columns] - moved, 0.0)

    gram_step()
    pl.semaphore_wait(barrier, len(partners))
    g_copy = send(g_ref, g_got, 0)
    s_copies = [send(s_ref.at[:, give], s_got[0], 0)]
    g_copy.wait_recv()
    pairs, small = 2 * rank, rank // 2
    sum_one[...] = g_ref[rank:, :] + g_got[rank:, :]
    tail = pl.ds(pl.multiple_of(rank + mine * rank, 8), rank)
    one_tail = send(sum_one.at[tail, pairs:], got_tail.at[tail], 1)
    one_cross = send(sum_one.at[:rank, pairs:], got_tail.at[:rank], 1)
    part = pl.ds(pl.multiple_of(rank + mine * small, 8), small)
    area = pl.ds(pl.multiple_of(mine * small, 8), small)
    near_copies = [
        send(sum_one.at[part, pairs:], near.at[0, area], 2),
        send(sum_one.at[part, pairs:], near.at[1, area], 1, 2),
    ]
    prepare(0, g_ref[:rank, :], g_got[:rank, :], slice(rank, None))
    solve(0, rows - rank)
    column_step(cot_loads, cot_in, k_ref, store_cot)
    k_copy = send(k_ref.at[:, give], k_got[0], 0)
    l_own[...] = s_ref[:rank, keep] - turned(g_ref[:rank, :pairs], z_own[0])[:rank]
    l_zero = s_got[0][:rank, :] - turned(g_got[:rank, :pairs], z_sib[0])[:rank]
    k_copy.wait_recv()
    k_sum[1][...] = k_ref[rank:, keep] + k_got[0][rank:, :]
    k_last_one = send(k_sum[1].at[pairs:], k_got[1].at[pairs:], 1)
    k_one = send(k_sum[1].at[:pairs], k_got[1].at[:pairs], 1)
    head = share((rows - rank) // 2)
    one_head = send(sum_one.at[head, :pairs], got_head.at[head], 1)
    one_cross.wait_recv()
    prepare(1, sum_one[:rank, pairs:], got_tail[:rank], slice(None))
    one_tail.wait_recv()
    tail_relay = relay(got_tail.at[tail])
    for copy in near_copies:
        copy.wait_recv()
    near_relay = relay(near.at[:, area])
    tail_relay.wait_recv()
    sum_two[...] = sum_one[rank:, pairs:] + got_tail[rank:]
    two_copy = send(sum_two.at[rank:], got_two.at[rank:], 2)
    solve(1, pairs)
    near_relay.wait_recv()
    got_two[:rank] = near[0] + near[1]
    prepare(2, sum_two[:rank], got_two[:rank], slice(rank, None))
    k_last_one.wait_recv()
    k_sum[3][...] = k_sum[1][pairs:] + k_got[1][pairs:]
    far_copies = [send(k_sum[3], far.at[0], 3), send(k_sum[3], far.at[1], 2, 3)]
    k_one.wait_recv()
    k_sum[2][:rank] = k_sum[1][rank:pairs] + k_got[1][rank:pairs]
    k_two = send(k_sum[2].at[:rank], k_got[2].at[:rank], 2)
    two_copy.wait_recv()
    sum_three[...] = sum_two[rank:] + got_two[rank:]
    three_copy = send(sum_three, got_three, 3)
    solve(2, rank)
    z_early = send(z_ship.at[: last * rank], z_out.at[: last * rank, keep], 0)
    one_head.wait_recv()
    head_relay = relay(got_head.at[head])
    row = slice(rank, 2 * rank)
    l_own[...] -= turned(g_ref[row, :pairs], z_own[1])[:rank]
    row = slice(2 * rank, 3 * rank)
    l_own[...] -= turned(g_ref[row, :pairs], z_own[2])[:rank]
    l_two = s_got[2][:rank, :] - turned(got_two[:rank], z_sib[2])[:rank]
    head_relay.wait_recv()
    row = slice(rank, 2 * rank)
    mixed = jnp.concatenate(
        [jnp.where(left_lanes, g_got[row, :pairs], 0.0), jnp.where(left_lanes, 0.0, got_head[:rank])], 0
    )
    change = turned(mixed, jnp.concatenate([z_own[1], z_sib[1]], 0))
    row = slice(2 * rank, 3 * rank)
    mixed = jnp.where(left_lanes, g_got[row, :pairs], got_head[rank : 2 * rank])
    change = change + turned(mixed, z_own[2])
    l_zero = l_zero - change[:rank]
    l_one = s_got[1][:rank, :] - change[rank:]
    z_early.wait_recv()
    move_early()
    k_two.wait_recv()
    for level in range(last):
        value = k_got[level][:rank, :] * scale
        k_out[block(level), keep] = value
        k_ship[block(level)] = k_ref[:rank, keep] * scale if level == 0 else value
    early = slice(0, last * rank)
    k_early = send(k_ship.at[early], k_out.at[early, keep], 0)
    three_copy.wait_recv()
    row = slice(3 * rank, 4 * rank)
    nothing = jnp.zeros((rank, pairs), jnp.float32)
    own = jnp.concatenate(
        [
            jnp.where(left_lanes, g_got[row, :pairs], got_head[2 * rank :]),
            jnp.where(left_lanes, got_two[rank:], 0.0),
            g_ref[row, :pairs],
        ],
        1,
    )
    sibling = jnp.concatenate([nothing, jnp.where(left_lanes, 0.0, got_three[...]), nothing], 1)
    prepare(3, own, sibling, slice(0, 5 * rank))
    change = solve(3, 5 * rank)
    z_late = send(z_ship.at[last * rank :], z_out.at[last * rank :, keep], 0)
    final = jnp.concatenate([l_zero, l_one, l_two, s_got[3][...]], 0) - change[: 4 * rank]
    l_out[:, keep] = final * scale
    l_ship[:rank] = (l_own[...] - change[4 * rank :]) * scale
    l_ship[rank:] = final[rank:] * scale
    l_copy = send(l_ship, l_out.at[:, keep], 0)
    for copy in far_copies:
        copy.wait_recv()
    value = (far[0] + far[1]) * scale
    k_out[block(last), keep] = value
    k_ship[block(last)] = value
    k_final = send(k_ship.at[block(last)], k_out.at[block(last), keep], 0)
    z_late.wait_recv()
    move_late(slice(None))
    l_copy.wait_recv()
    k_early.wait_recv()
    k_final.wait_recv()
    for copy in sends:
        copy.wait_send()


def tree_steps(
    levels, rank, base, steps, s_ref, k_ref, g_ref, node_ref, z_out, l_out, k_out, scratch
):
    inverse = scratch[0]
    own = [None] + [scratch[1 + 3 * n : 4 + 3 * n] for n in range(levels - 1)]
    start = 1 + 3 * (levels - 1)
    got = [scratch[start + 3 * n : start + 3 * n + 3] for n in range(levels)]
    start += 3 * levels
    packed, other, node_sem, send_sem, recv_sem = scratch[start:]
    cols = s_ref.shape[1]
    half = cols // 2
    position = lax.axis_index("leaf")

    def bit_of(height):
        return lax.rem(lax.div(position, 2 ** (base + height)), 2)

    def partner(height):
        return position + (1 - 2 * bit_of(height)) * 2 ** (base + height)

    fetches = []
    for height in range(levels):
        offset = 2**levels - 2 ** (levels - height)
        node = offset + lax.div(position, 2 ** (base + height + 1))
        fetch = pltpu.make_async_copy(node_ref.at[node], inverse.at[height], node_sem.at[height])
        fetch.start()
        fetches.append(fetch)

    barrier = pltpu.get_barrier_semaphore()
    for height in range(levels):
        pl.semaphore_signal(
            barrier, inc=1, device_id={"leaf": partner(height)}, device_id_type=MESH
        )
    steps[0]()
    pl.semaphore_wait(barrier, levels)

    def send(source, target, height, slot):
        copy = pltpu.make_async_remote_copy(
            src_ref=source,
            dst_ref=target,
            send_sem=send_sem.at[slot],
            recv_sem=recv_sem.at[slot],
            device_id={"leaf": partner(height)},
            device_id_type=MESH,
        )
        copy.start()
        return copy

    mine = bit_of(0)
    keep = pl.ds(pl.multiple_of(mine * half, half), half)
    give = pl.ds(pl.multiple_of((1 - mine) * half, half), half)
    s_all = [s_ref.at[:, keep]] + [own[n][0] for n in range(1, levels)]
    g_all = [g_ref] + [own[n][1] for n in range(1, levels)]
    k_all = [k_ref.at[:, keep]] + [own[n][2] for n in range(1, levels)]
    sends = []

    def half_rows(height):
        size = g_all[height].shape[0] // 2
        return pl.ds(pl.multiple_of(mine * size, 8), size)

    def advance_gram(height, copy):
        copy.wait_recv()
        if 0 < height < levels - 1:
            area = got[height][1].at[half_rows(height), :]
            relay = send(area, area, 0, 3 * levels + 2 + height)
            sends.append(relay)
            relay.wait_recv()
        if height == levels - 1:
            return None
        g_now, g_got, g_next = g_all[height], got[height][1], g_all[height + 1]
        skip = g_now.shape[1] - g_next.shape[1]
        g_next[...] = g_now[rank:, skip:] + g_got[rank:, skip:]
        source, target = g_next, got[height + 1][1]
        if height < levels - 2:
            area = half_rows(height + 1)
            source, target = source.at[area, :], target.at[area, :]
        sends.append(send(source, target, height + 1, 3 * height + 4))
        return sends[-1]

    g_copy = send(g_ref, got[0][1], 0, 1)
    sends.append(g_copy)
    steps[1]()
    s_copy = send(s_ref.at[:, give], got[0][0], 0, 0)
    sends.append(s_copy)
    g_copy = advance_gram(0, g_copy)
    steps[2]()
    k_copy = send(k_ref.at[:, give], got[0][2], 0, 2)
    sends.append(k_copy)
    z_own, z_sib = [], []
    for height in range(levels):
        shift = rank * height - rank * height // 128 * 128
        s_now, g_now, k_now = s_all[height], g_all[height], k_all[height]
        s_got, g_got, k_got = got[height]
        s_copy.wait_recv()
        lower = bit_of(height) == 0
        here, there = s_now[:rank, :], s_got[:rank, :]
        pair = jnp.concatenate(
            [jnp.where(lower, here, there), jnp.where(lower, there, here)], 0
        )
        fetches[height].wait()
        z = dot(inverse[height], pair)
        z_own.append(jnp.where(lower, z[:rank], z[rank:]))
        z_sib.append(jnp.where(lower, z[rank:], z[:rank]))
        if height < levels - 1:
            s_next, _, k_next = own[height + 1]
            block = slice(shift, shift + rank)
            s_next[...] = (
                s_now[rank:, :]
                + s_got[rank:, :]
                - dot(g_now[rank:, :][:, block], z_own[-1])
                - dot(g_got[rank:, :][:, block], z_sib[-1])
            )
            s_copy = send(s_next, got[height + 1][0], height + 1, 3 * height + 3)
            sends.append(s_copy)
            k_copy.wait_recv()
            k_next[...] = k_now[rank:, :] + k_got[rank:, :]
            k_copy = send(k_next, got[height + 1][2], height + 1, 3 * height + 5)
            sends.append(k_copy)
            g_copy = advance_gram(height + 1, g_copy)
    rows = levels * rank
    scale = 1.0 / math.sqrt(cols)
    z_all = jnp.concatenate(z_own, 0)
    areas = [pl.ds(n * rows, rows) for n in range(3)]
    packed[:rank, :] = z_sib[0]
    packed[rank:rows, :] = z_all[rank:]
    last = [send(packed.at[areas[0]], other.at[areas[0]], 0, 3 * levels)]
    z_out[:, keep] = z_all
    l_first = (s_ref[:rank, keep] - dot(g_ref[:rank, :], z_all)) * scale
    packed[rows : rows + rank, :] = l_first
    for height in range(levels):
        shift = rank * height - rank * height // 128 * 128
        part = slice(height * rank, (height + 1) * rank)
        chain = jnp.concatenate([z_sib[height]] + z_own[height + 1 :], 0)
        row = got[height][1][:rank, :][:, shift:]
        l_part = (got[height][0][:rank, :] - dot(row, chain)) * scale
        l_out[part, keep] = l_part
        if height > 0:
            packed[rows + height * rank : rows + (height + 1) * rank, :] = l_part
    last.append(send(packed.at[areas[1]], other.at[areas[1]], 0, 3 * levels + 1))
    k_copy.wait_recv()
    packed[2 * rows : 2 * rows + rank, :] = k_ref[:rank, keep] * scale
    for height in range(levels):
        part = slice(height * rank, (height + 1) * rank)
        k_part = got[height][2][:rank, :] * scale
        k_out[part, keep] = k_part
        if height > 0:
            packed[2 * rows + height * rank : 2 * rows + (height + 1) * rank, :] = k_part
    last.append(send(packed.at[areas[2]], other.at[areas[2]], 0, 3 * levels + 2))
    for copy, target, area in zip(last, (z_out, l_out, k_out), areas):
        copy.wait_recv()
        target[:, give] = other[area, :]
    for copy in sends + last:
        copy.wait_send()


def tree_scratch(levels, rank, rows, cols, node_shape):
    half = cols // 2
    own, got = [], []
    for height in range(levels):
        left = rows - rank * height
        wide = rows - rank * height // 128 * 128
        group = [
            pltpu.VMEM((left, half), jnp.float32),
            pltpu.VMEM((left, wide), jnp.float32),
            pltpu.VMEM((left, half), jnp.float32),
        ]
        got += group
        if height > 0:
            own += group
    count = 4 * levels + 1
    return (
        [pltpu.VMEM((levels,) + node_shape, jnp.float32)]
        + own
        + got
        + [
            pltpu.VMEM((3 * rows, half), jnp.float32),
            pltpu.VMEM((3 * rows, half), jnp.float32),
            pltpu.SemaphoreType.DMA((levels,)),
            pltpu.SemaphoreType.DMA((count,)),
            pltpu.SemaphoreType.DMA((count,)),
        ]
    )


def tree(sums, weight_sums, gram, node_inverse, levels, rank, base):
    rows, cols = sums.shape
    vmem = pl.BlockSpec(memory_space=pltpu.VMEM)
    return pl.pallas_call(
        functools.partial(tree_kernel, levels, rank, base),
        out_shape=[jax.ShapeDtypeStruct((rows, cols), jnp.float32)] * 3,
        in_specs=[vmem] * 3 + [pl.BlockSpec(memory_space=pl.ANY)],
        out_specs=[vmem] * 3,
        scratch_shapes=tree_scratch(levels, rank, rows, cols, node_inverse.shape[1:]),
        compiler_params=pltpu.CompilerParams(collective_id=0, has_side_effects=True),
    )(sums, weight_sums, gram, node_inverse)


def whole_tree(leaf_rows, right_side, cotangent, basis, saved, node_inverse, levels, rank, tile):
    rows, depth = basis.shape
    cols = right_side.shape[1]
    vmem = pl.BlockSpec(memory_space=pltpu.VMEM)
    hbm = pl.BlockSpec(memory_space=pltpu.HBM)
    args = (right_side, cotangent, basis, saved, node_inverse)
    shapes = (
        [((rows, cols), jnp.float32)] * 2
        + [((depth, cols), jnp.float32)]
        + [((depth, cols), jnp.bfloat16)] * 2
    )
    return pl.pallas_call(
        functools.partial(whole_kernel, levels, rank, tile),
        out_shape=[pltpu.VMEM(shape, dtype) for shape, dtype in shapes],
        in_specs=[pl.BlockSpec(memory_space=pltpu.SMEM)] + [hbm] * 5,
        out_specs=[vmem] * 5,
        scratch_shapes=whole_scratch(levels, rank, rows, cols, depth, depth // tile),
        compiler_params=pltpu.CompilerParams(
            collective_id=0, has_side_effects=True, vmem_limit_bytes=VMEM_TREE
        ),
    )(leaf_rows, *[pltpu.with_memory_space_constraint(arg, pltpu.HBM) for arg in args])


def whole_scratch(levels, rank, rows, cols, depth, tiles):
    half, pairs = cols // 2, 2 * rank

    def full(*shape):
        return pltpu.VMEM(shape, jnp.float32)

    def short(*shape):
        return pltpu.VMEM(shape, jnp.bfloat16)

    steps = [full(rows - rank * height, half) for height in range(levels)]
    return (
        [full(rows, cols), short(rows, depth), short(rows, depth)]
        + [full(rows, cols), full(rows, cols), full(rows, rows), full(rows, rows)]
        + [full(depth, cols)]
        + [full(rows, depth)] * 2
        + [short(rows, depth)] * 2
        + [full(levels, pairs, pairs)]
        + [short(pairs + rows + pairs, pairs)] * 2
        + [full(rank, half)]
        + [full(rows, half)] * 3
        + [
            pltpu.SemaphoreType.DMA((4, tiles)),
            pltpu.SemaphoreType.DMA((levels,)),
            pltpu.SemaphoreType.DMA((SLOTS,)),
            pltpu.SemaphoreType.DMA((SLOTS,)),
        ]
        + steps * 4
        + [
            full(rows - rank, rows),
            full(rows - rank, pairs),
            full(rows - rank, pairs),
            full(pairs, pairs),
            full(pairs, pairs),
            full(rank, pairs),
            full(rank, pairs),
            full(2, rank, pairs),
            full(2, rank, half),
        ]
    )


def finish_kernel(
    tile,
    rows_ref,
    l_ref,
    k_ref,
    x_ref,
    cot_high,
    cot_low,
    x_hbm,
    left_hbm,
    grad_hbm,
    left_ref,
    grad_ref,
    sem,
):
    tiles = x_ref.shape[0] // tile
    copies = []

    def out(source, target, index, kind, n):
        copy = pltpu.make_async_copy(source.at[index], target.at[index], sem.at[kind, n])
        copy.start()
        copies.append(copy)

    left, right = split(l_ref[...]), split(k_ref[...])
    for n in range(tiles):
        out(x_ref, x_hbm, (slice(n * tile, (n + 1) * tile), slice(None)), 0, n)
    for n in range(tiles):
        part = slice(n * tile, (n + 1) * tile)
        down, across = (part, slice(None)), (slice(None), part)
        value = triple(left, (cot_high[down], cot_low[down]), ((1,), (1,)))
        live = n * tile + lax.broadcasted_iota(jnp.int32, (1, tile), 1) < rows_ref[0]
        left_ref[across] = jnp.where(live, value, 0.0).astype(jnp.bfloat16)
        out(left_ref, left_hbm, across, 1, n)
        value = triple(right, split(x_ref[down]), ((1,), (1,)))
        grad_ref[across] = value.astype(jnp.bfloat16)
        out(grad_ref, grad_hbm, across, 2, n)
    for copy in copies:
        copy.wait()


def finish(leaf_rows, parts, tile):
    depth, cols = parts[2].shape
    rows = parts[0].shape[0]
    vmem = pl.BlockSpec(memory_space=pltpu.VMEM)
    hbm = pl.BlockSpec(memory_space=pltpu.HBM)
    shapes = [
        ((depth, cols), jnp.float32),
        ((rows, depth), jnp.bfloat16),
        ((rows, depth), jnp.bfloat16),
    ]
    return pl.pallas_call(
        functools.partial(finish_kernel, tile),
        out_shape=[pltpu.HBM(shape, dtype) for shape, dtype in shapes],
        in_specs=[pl.BlockSpec(memory_space=pltpu.SMEM)] + [vmem] * 5,
        out_specs=[hbm] * 3,
        scratch_shapes=[pltpu.VMEM(shape, dtype) for shape, dtype in shapes[1:]]
        + [pltpu.SemaphoreType.DMA((3, depth // tile))],
        compiler_params=pltpu.CompilerParams(vmem_limit_bytes=VMEM_FINISH),
    )(leaf_rows, *[pltpu.with_memory_space_constraint(part, pltpu.VMEM) for part in parts])


def split(value):
    high = value.astype(jnp.bfloat16)
    return high, (value - high.astype(jnp.float32)).astype(jnp.bfloat16)


def triple(left, right, dims):
    def one(a, b):
        return lax.dot_general(a, b, (dims, ((), ())), preferred_element_type=jnp.float32)

    return one(left[0], right[1]) + one(left[1], right[0]) + one(left[0], right[0])


def lead_kernel(rows_ref, right_ref, cot_ref, basis_ref, saved_ref, s_ref, k_ref, g_ref):
    step = pl.program_id(0)
    tile = basis_ref.shape[1]
    place = step * tile + lax.broadcasted_iota(jnp.int32, (1, tile), 1)
    basis = split(jnp.where(place < rows_ref[0], basis_ref[...], 0.0))
    s_now = triple(basis, split(right_ref[...]), ((1,), (0,)))
    k_now = triple(basis, split(cot_ref[...]), ((1,), (0,)))
    g_now = triple(basis, split(saved_ref[...]), ((1,), (1,)))

    @pl.when(step == 0)
    def _():
        s_ref[...] = s_now
        k_ref[...] = k_now
        g_ref[...] = g_now

    @pl.when(step > 0)
    def _():
        s_ref[...] += s_now
        k_ref[...] += k_now
        g_ref[...] += g_now


def close_kernel(
    rows_ref, right_ref, cot_ref, saved_ref, z_ref, l_ref, k_ref, x_ref, left_ref, grad_ref
):
    tile = saved_ref.shape[1]
    first = pl.program_id(0) * tile
    down = first + lax.broadcasted_iota(jnp.int32, (tile, 1), 0)
    across = first + lax.broadcasted_iota(jnp.int32, (1, tile), 1)
    moved = triple(split(saved_ref[...]), split(z_ref[...]), ((0,), (0,)))
    solved = jnp.where(down < rows_ref[0], right_ref[...] - moved, 0.0)
    x_ref[...] = solved
    left = triple(split(l_ref[...]), split(cot_ref[...]), ((1,), (1,)))
    left_ref[...] = jnp.where(across < rows_ref[0], left, 0.0).astype(jnp.bfloat16)
    grad = triple(split(k_ref[...]), split(solved), ((1,), (1,)))
    grad_ref[...] = grad.astype(jnp.bfloat16)


def body(right_side, cotangent, coeff_basis, saved_basis, node_inverse, leaf_rows):
    row_count, cols = right_side.shape
    levels, rank = coeff_basis.shape[0], coeff_basis.shape[1]
    height = levels * rank
    base = lax.axis_size("leaf").bit_length() - 1 - levels
    basis = coeff_basis.reshape(height, row_count)
    saved = saved_basis.reshape(height, row_count)
    tile = math.gcd(row_count, TILE)
    grid = (row_count // tile,)
    count = pl.BlockSpec(memory_space=pltpu.SMEM)
    tall = pl.BlockSpec((tile, cols), lambda i: (i, 0))
    wide = pl.BlockSpec((height, tile), lambda i: (0, i))
    small = pl.BlockSpec((height, cols), lambda i: (0, 0))
    square = pl.BlockSpec((height, height), lambda i: (0, 0))
    if base == 0:
        parts = whole_tree(
            leaf_rows, right_side, cotangent, basis, saved, node_inverse, levels, rank, tile
        )
        current, left, right = finish(leaf_rows, parts, tile)
    else:
        sums, weight_sums, gram = pl.pallas_call(
            lead_kernel,
            grid=grid,
            out_shape=[
                jax.ShapeDtypeStruct((height, cols), jnp.float32),
                jax.ShapeDtypeStruct((height, cols), jnp.float32),
                jax.ShapeDtypeStruct((height, height), jnp.float32),
            ],
            in_specs=[count, tall, tall, wide, wide],
            out_specs=[small, small, square],
        )(leaf_rows, right_side, cotangent, basis, saved)
        for bit in range(base):
            sums = sums + swapped(sums, bit)
            weight_sums = weight_sums + swapped(weight_sums, bit)
            gram = gram + swapped(gram, bit)
        z_own, l_sib, k_sib = tree(sums, weight_sums, gram, node_inverse, levels, rank, base)
        current, left, right = pl.pallas_call(
            close_kernel,
            grid=grid,
            out_shape=[
                jax.ShapeDtypeStruct((row_count, cols), jnp.float32),
                jax.ShapeDtypeStruct((height, row_count), jnp.bfloat16),
                jax.ShapeDtypeStruct((height, row_count), jnp.bfloat16),
            ],
            in_specs=[count, tall, tall, wide, small, small, small],
            out_specs=[tall, wide, wide],
        )(leaf_rows, right_side, cotangent, saved, z_own, l_sib, k_sib)
    shape = (levels, rank, row_count)
    return current, left.reshape(shape), right.reshape(shape)


def solution(mesh):
    in_specs = (
        P(("groups", "leaf"), None),
        P(("groups", "leaf"), None),
        P(None, None, ("groups", "leaf")),
        P(None, None, ("groups", "leaf")),
        P("groups", None, None),
        P(("groups", "leaf")),
    )
    out_specs = (
        P(("groups", "leaf"), None),
        P(None, None, ("groups", "leaf")),
        P(None, None, ("groups", "leaf")),
    )
    return jax.shard_map(body, mesh=mesh, in_specs=in_specs, out_specs=out_specs, check_vma=False)
```

```python
import functools
import math

import jax
import jax.numpy as jnp
from jax import lax
from jax.experimental import pallas as pl
from jax.experimental.pallas import tpu as pltpu
from jax.sharding import PartitionSpec as P

MESH = pl.DeviceIdType.MESH
TILE = 512
SLOTS = 32
VMEM_TREE = 32 * 2**20
VMEM_FINISH = 16 * 2**20


def swapped(value, bit):
    mask = 2**bit
    pairs = [(source, source ^ mask) for source in range(lax.axis_size("leaf"))]
    return lax.ppermute(value, "leaf", pairs)


def dot(a, b, dims=((1,), (0,))):
    return triple(split(a), split(b), dims)


def tree_kernel(
    levels, rank, base, s_ref, k_ref, g_ref, node_ref, z_out, l_out, k_out, *scratch
):
    steps = [lambda: None] * 3
    tree_steps(
        levels, rank, base, steps, s_ref, k_ref, g_ref, node_ref, z_out, l_out, k_out, scratch
    )


def whole_kernel(
    levels,
    rank,
    tile,
    rows_ref,
    right_ref,
    cot_ref,
    basis_ref,
    saved_ref,
    node_ref,
    l_out,
    k_out,
    right_in,
    cot_high,
    cot_low,
    z_out,
    saved_high,
    saved_low,
    s_ref,
    k_ref,
    g_ref,
    g_got,
    cot_in,
    basis_in,
    saved_in,
    high_ref,
    low_ref,
    inverse,
    mix_high,
    mix_low,
    l_own,
    l_ship,
    k_ship,
    z_ship,
    load_sem,
    node_sem,
    send_sem,
    recv_sem,
    *scratch,
):
    depth = basis_ref.shape[1]
    rows, cols = s_ref.shape
    half = cols // 2
    last = levels - 1
    tiles = depth // tile
    scale = 1.0 / math.sqrt(cols)
    position = lax.axis_index("leaf")
    s_got, s_sum, k_got, k_sum = [list(scratch[levels * n : levels * (n + 1)]) for n in range(4)]
    sum_one, got_tail, got_head, sum_two, got_two, sum_three, got_three, near, far = scratch[4 * levels :]

    def bit_of(height):
        return lax.rem(lax.div(position, 2**height), 2)

    def partner(*heights):
        return position + sum((1 - 2 * bit_of(height)) * 2**height for height in heights)

    def block(level, base=0):
        return slice((level - base) * rank, (level - base + 1) * rank)

    def load(source, target, kind, axis):
        copies = []
        for n in range(tiles):
            part = pl.ds(n * tile, tile)
            index = (part, slice(None)) if axis == 0 else (slice(None), part)
            copies.append(
                pltpu.make_async_copy(source.at[index], target.at[index], load_sem.at[kind, n])
            )
        return copies

    basis_loads = load(basis_ref, basis_in, 0, 1)
    saved_loads = load(saved_ref, saved_in, 1, 1)
    right_loads = load(right_ref, right_in, 2, 0)
    cot_loads = load(cot_ref, cot_in, 3, 0)
    for loads in zip(basis_loads, saved_loads, right_loads):
        for one_load in loads:
            one_load.start()
    for one_load in cot_loads:
        one_load.start()
    fetches = []
    for height in range(levels):
        offset = 2**levels - 2 ** (levels - height)
        node = offset + lax.div(position, 2 ** (height + 1))
        fetch = pltpu.make_async_copy(node_ref.at[node], inverse.at[height], node_sem.at[height])
        fetch.start()
        fetches.append(fetch)

    barrier = pltpu.get_barrier_semaphore()
    partners = [(height,) for height in range(levels)] + [(1, 2), (2, 3)]
    for heights in partners:
        pl.semaphore_signal(
            barrier, inc=1, device_id={"leaf": partner(*heights)}, device_id_type=MESH
        )

    sends = []

    def send(source, target, *heights):
        slot = len(sends)
        copy = pltpu.make_async_remote_copy(
            src_ref=source,
            dst_ref=target,
            send_sem=send_sem.at[slot],
            recv_sem=recv_sem.at[slot],
            device_id={"leaf": partner(*heights)},
            device_id_type=MESH,
        )
        copy.start()
        sends.append(copy)
        return copy

    mine = bit_of(0)
    keep = pl.ds(pl.multiple_of(mine * half, half), half)
    give = pl.ds(pl.multiple_of((1 - mine) * half, half), half)

    def gram_step():
        total, sums = None, None
        for n in range(tiles):
            part = slice(n * tile, (n + 1) * tile)
            live = n * tile + lax.broadcasted_iota(jnp.int32, (1, tile), 1) < rows_ref[0]
            basis_loads[n].wait()
            saved_loads[n].wait()
            right_loads[n].wait()
            basis = split(jnp.where(live, basis_in[:, part], 0.0))
            high_ref[:, part], low_ref[:, part] = basis
            saved = split(saved_in[:, part])
            saved_high[:, part], saved_low[:, part] = saved
            term = triple(saved, basis, ((1,), (1,)))
            total = term if total is None else total + term
            term = triple(basis, split(right_in[part, :]), ((1,), (0,)))
            sums = term if sums is None else sums + term
        g_ref[...] = total
        s_ref[...] = sums

    def column_step(loads, source, target, store):
        for one_load in loads:
            one_load.wait()
        total = None
        for n in range(tiles):
            part = slice(n * tile, (n + 1) * tile)
            pair = split(source[part, :])
            store(part, pair)
            term = triple((high_ref[:, part], low_ref[:, part]), pair, ((1,), (0,)))
            total = term if total is None else total + term
        target[...] = total

    def store_right(part, pair):
        pass

    def store_cot(part, pair):
        cot_high[part, :], cot_low[part, :] = pair

    lane = lax.broadcasted_iota(jnp.int32, (1, 2 * rank), 1)
    left_lanes = lane < rank

    def order(height, own, sibling):
        lower = bit_of(height) == 0
        return jnp.concatenate(
            [jnp.where(lower, own, sibling), jnp.where(lower, sibling, own)], 0
        )

    def prepare(height, own, sibling, part):
        fetches[height].wait()
        node = inverse[height]
        cross = dot(order(height, own, sibling), node, ((0,), (0,)))[part]
        high, low = split(jnp.concatenate([node, cross], 0))
        mix_high[: high.shape[0]] = high
        mix_low[: low.shape[0]] = low

    z_own, z_sib = [], []

    def solve(height, count):
        own = s_ref[:, keep] if height == 0 else s_sum[height][...]
        s_copies[0].wait_recv()
        pair = order(height, own[:rank], s_got[height][:rank, :])
        high, low = split(pair)
        size = 2 * rank + count
        wide = one(mix_high[:size], jnp.concatenate([high, low], 1))
        out = wide[:, :half] + wide[:, half:] + one(mix_low[:size], high)
        lower = bit_of(height) == 0
        z_own.append(jnp.where(lower, out[:rank], out[rank : 2 * rank]))
        z_sib.append(jnp.where(lower, out[rank : 2 * rank], out[:rank]))
        change = out[2 * rank :]
        if height < last:
            for copy in s_copies[1:]:
                copy.wait_recv()
            following = own[rank:] + s_got[height][rank:, :] - change
            s_sum[height + 1][...] = following
            target = s_got[height + 1]
            source = s_sum[height + 1]
            s_copies[:] = [send(source, target, height + 1)]
        z_out[block(height), keep] = z_own[-1]
        z_ship[block(height)] = z_sib[-1] if height == 0 else z_own[-1]
        return change

    def one(a, b):
        return lax.dot_general(
            a, b, (((1,), (0,)), ((), ())), preferred_element_type=jnp.float32
        )

    def turned(a, b):
        return dot(a, b, ((0,), (0,)))

    def share(size):
        return pl.ds(pl.multiple_of(mine * size, 8), size)

    def relay(area):
        return send(area, area, 0)

    def move_early():
        z = split(z_out[: last * rank, :])
        for n in range(tiles):
            part = slice(n * tile, (n + 1) * tile)
            saved = (saved_high[: last * rank, part], saved_low[: last * rank, part])
            right_in[part, :] -= triple(saved, z, ((0,), (0,)))

    def move_late(columns):
        high, low = split(z_out[last * rank :, columns])
        stacked = jnp.concatenate([high, high, low], 0)
        for n in range(tiles):
            part = slice(n * tile, (n + 1) * tile)
            saved = saved_high[last * rank :, part]
            saved = jnp.concatenate([saved, saved_low[last * rank :, part], saved], 0)
            moved = lax.dot_general(
                saved, stacked, (((0,), (0,)), ((), ())), preferred_element_type=jnp.float32
            )
            live = n * tile + lax.broadcasted_iota(jnp.int32, (tile, 1), 0) < rows_ref[0]
            right_in[part, columns] = jnp.where(live, right_in[part, columns] - moved, 0.0)

    gram_step()
    pl.semaphore_wait(barrier, len(partners))
    g_copy = send(g_ref, g_got, 0)
    s_copies = [send(s_ref.at[:, give], s_got[0], 0)]
    g_copy.wait_recv()
    pairs, small = 2 * rank, rank // 2
    sum_one[...] = g_ref[rank:, :] + g_got[rank:, :]
    tail = pl.ds(pl.multiple_of(rank + mine * rank, 8), rank)
    one_tail = send(sum_one.at[tail, pairs:], got_tail.at[tail], 1)
    part = pl.ds(pl.multiple_of(rank + mine * small, 8), small)
    area = pl.ds(pl.multiple_of(mine * small, 8), small)
    near_copies = [
        send(sum_one.at[part, pairs:], near.at[0, area], 2),
        send(sum_one.at[part, pairs:], near.at[1, area], 1, 2),
    ]
    prepare(0, g_ref[:rank, :], g_got[:rank, :], slice(rank, None))
    one_cross = send(sum_one.at[:rank, pairs:], got_tail.at[:rank], 1)
    solve(0, rows - rank)
    column_step(cot_loads, cot_in, k_ref, store_cot)
    k_copy = send(k_ref.at[:, give], k_got[0], 0)
    l_own[...] = s_ref[:rank, keep] - turned(g_ref[:rank, :pairs], z_own[0])[:rank]
    l_zero = s_got[0][:rank, :] - turned(g_got[:rank, :pairs], z_sib[0])[:rank]
    k_copy.wait_recv()
    k_sum[1][...] = k_ref[rank:, keep] + k_got[0][rank:, :]
    k_last_one = send(k_sum[1].at[pairs:], k_got[1].at[pairs:], 1)
    k_one = send(k_sum[1].at[:pairs], k_got[1].at[:pairs], 1)
    head = share((rows - rank) // 2)
    one_head = send(sum_one.at[head, :pairs], got_head.at[head], 1)
    one_cross.wait_recv()
    prepare(1, sum_one[:rank, pairs:], got_tail[:rank], slice(None))
    one_tail.wait_recv()
    tail_relay = relay(got_tail.at[tail])
    for copy in near_copies:
        copy.wait_recv()
    near_relay = relay(near.at[:, area])
    tail_relay.wait_recv()
    sum_two[...] = sum_one[rank:, pairs:] + got_tail[rank:]
    two_copy = send(sum_two.at[rank:], got_two.at[rank:], 2)
    solve(1, pairs)
    near_relay.wait_recv()
    got_two[:rank] = near[0] + near[1]
    prepare(2, sum_two[:rank], got_two[:rank], slice(rank, None))
    k_last_one.wait_recv()
    k_sum[3][...] = k_sum[1][pairs:] + k_got[1][pairs:]
    far_copies = [send(k_sum[3], far.at[0], 3), send(k_sum[3], far.at[1], 2, 3)]
    k_one.wait_recv()
    k_sum[2][:rank] = k_sum[1][rank:pairs] + k_got[1][rank:pairs]
    k_two = send(k_sum[2].at[:rank], k_got[2].at[:rank], 2)
    two_copy.wait_recv()
    sum_three[...] = sum_two[rank:] + got_two[rank:]
    three_copy = send(sum_three, got_three, 3)
    solve(2, rank)
    z_early = send(z_ship.at[: last * rank], z_out.at[: last * rank, keep], 0)
    one_head.wait_recv()
    head_relay = relay(got_head.at[head])
    row = slice(rank, 2 * rank)
    l_own[...] -= turned(g_ref[row, :pairs], z_own[1])[:rank]
    row = slice(2 * rank, 3 * rank)
    l_own[...] -= turned(g_ref[row, :pairs], z_own[2])[:rank]
    l_two = s_got[2][:rank, :] - turned(got_two[:rank], z_sib[2])[:rank]
    head_relay.wait_recv()
    row = slice(rank, 2 * rank)
    mixed = jnp.concatenate(
        [jnp.where(left_lanes, g_got[row, :pairs], 0.0), jnp.where(left_lanes, 0.0, got_head[:rank])], 0
    )
    change = turned(mixed, jnp.concatenate([z_own[1], z_sib[1]], 0))
    row = slice(2 * rank, 3 * rank)
    mixed = jnp.where(left_lanes, g_got[row, :pairs], got_head[rank : 2 * rank])
    change = change + turned(mixed, z_own[2])
    l_zero = l_zero - change[:rank]
    l_one = s_got[1][:rank, :] - change[rank:]
    z_early.wait_recv()
    move_early()
    k_two.wait_recv()
    for level in range(last):
        value = k_got[level][:rank, :] * scale
        k_out[block(level), keep] = value
        k_ship[block(level)] = k_ref[:rank, keep] * scale if level == 0 else value
    early = slice(0, last * rank)
    k_early = send(k_ship.at[early], k_out.at[early, keep], 0)
    three_copy.wait_recv()
    row = slice(3 * rank, 4 * rank)
    nothing = jnp.zeros((rank, pairs), jnp.float32)
    own = jnp.concatenate(
        [
            jnp.where(left_lanes, g_got[row, :pairs], got_head[2 * rank :]),
            jnp.where(left_lanes, got_two[rank:], 0.0),
            g_ref[row, :pairs],
        ],
        1,
    )
    sibling = jnp.concatenate([nothing, jnp.where(left_lanes, 0.0, got_three[...]), nothing], 1)
    prepare(3, own, sibling, slice(0, 5 * rank))
    change = solve(3, 5 * rank)
    z_late = send(z_ship.at[last * rank :], z_out.at[last * rank :, keep], 0)
    final = jnp.concatenate([l_zero, l_one, l_two, s_got[3][...]], 0) - change[: 4 * rank]
    l_out[:, keep] = final * scale
    l_ship[:rank] = (l_own[...] - change[4 * rank :]) * scale
    l_ship[rank:] = final[rank:] * scale
    l_copy = send(l_ship, l_out.at[:, keep], 0)
    for copy in far_copies:
        copy.wait_recv()
    value = (far[0] + far[1]) * scale
    k_out[block(last), keep] = value
    k_ship[block(last)] = value
    k_final = send(k_ship.at[block(last)], k_out.at[block(last), keep], 0)
    z_late.wait_recv()
    move_late(slice(None))
    l_copy.wait_recv()
    k_early.wait_recv()
    k_final.wait_recv()
    for copy in sends:
        copy.wait_send()


def tree_steps(
    levels, rank, base, steps, s_ref, k_ref, g_ref, node_ref, z_out, l_out, k_out, scratch
):
    inverse = scratch[0]
    own = [None] + [scratch[1 + 3 * n : 4 + 3 * n] for n in range(levels - 1)]
    start = 1 + 3 * (levels - 1)
    got = [scratch[start + 3 * n : start + 3 * n + 3] for n in range(levels)]
    start += 3 * levels
    packed, other, node_sem, send_sem, recv_sem = scratch[start:]
    cols = s_ref.shape[1]
    half = cols // 2
    position = lax.axis_index("leaf")

    def bit_of(height):
        return lax.rem(lax.div(position, 2 ** (base + height)), 2)

    def partner(height):
        return position + (1 - 2 * bit_of(height)) * 2 ** (base + height)

    fetches = []
    for height in range(levels):
        offset = 2**levels - 2 ** (levels - height)
        node = offset + lax.div(position, 2 ** (base + height + 1))
        fetch = pltpu.make_async_copy(node_ref.at[node], inverse.at[height], node_sem.at[height])
        fetch.start()
        fetches.append(fetch)

    barrier = pltpu.get_barrier_semaphore()
    for height in range(levels):
        pl.semaphore_signal(
            barrier, inc=1, device_id={"leaf": partner(height)}, device_id_type=MESH
        )
    steps[0]()
    pl.semaphore_wait(barrier, levels)

    def send(source, target, height, slot):
        copy = pltpu.make_async_remote_copy(
            src_ref=source,
            dst_ref=target,
            send_sem=send_sem.at[slot],
            recv_sem=recv_sem.at[slot],
            device_id={"leaf": partner(height)},
            device_id_type=MESH,
        )
        copy.start()
        return copy

    mine = bit_of(0)
    keep = pl.ds(pl.multiple_of(mine * half, half), half)
    give = pl.ds(pl.multiple_of((1 - mine) * half, half), half)
    s_all = [s_ref.at[:, keep]] + [own[n][0] for n in range(1, levels)]
    g_all = [g_ref] + [own[n][1] for n in range(1, levels)]
    k_all = [k_ref.at[:, keep]] + [own[n][2] for n in range(1, levels)]
    sends = []

    def half_rows(height):
        size = g_all[height].shape[0] // 2
        return pl.ds(pl.multiple_of(mine * size, 8), size)

    def advance_gram(height, copy):
        copy.wait_recv()
        if 0 < height < levels - 1:
            area = got[height][1].at[half_rows(height), :]
            relay = send(area, area, 0, 3 * levels + 2 + height)
            sends.append(relay)
            relay.wait_recv()
        if height == levels - 1:
            return None
        g_now, g_got, g_next = g_all[height], got[height][1], g_all[height + 1]
        skip = g_now.shape[1] - g_next.shape[1]
        g_next[...] = g_now[rank:, skip:] + g_got[rank:, skip:]
        source, target = g_next, got[height + 1][1]
        if height < levels - 2:
            area = half_rows(height + 1)
            source, target = source.at[area, :], target.at[area, :]
        sends.append(send(source, target, height + 1, 3 * height + 4))
        return sends[-1]

    g_copy = send(g_ref, got[0][1], 0, 1)
    sends.append(g_copy)
    steps[1]()
    s_copy = send(s_ref.at[:, give], got[0][0], 0, 0)
    sends.append(s_copy)
    g_copy = advance_gram(0, g_copy)
    steps[2]()
    k_copy = send(k_ref.at[:, give], got[0][2], 0, 2)
    sends.append(k_copy)
    z_own, z_sib = [], []
    for height in range(levels):
        shift = rank * height - rank * height // 128 * 128
        s_now, g_now, k_now = s_all[height], g_all[height], k_all[height]
        s_got, g_got, k_got = got[height]
        s_copy.wait_recv()
        lower = bit_of(height) == 0
        here, there = s_now[:rank, :], s_got[:rank, :]
        pair = jnp.concatenate(
            [jnp.where(lower, here, there), jnp.where(lower, there, here)], 0
        )
        fetches[height].wait()
        z = dot(inverse[height], pair)
        z_own.append(jnp.where(lower, z[:rank], z[rank:]))
        z_sib.append(jnp.where(lower, z[rank:], z[:rank]))
        if height < levels - 1:
            s_next, _, k_next = own[height + 1]
            block = slice(shift, shift + rank)
            s_next[...] = (
                s_now[rank:, :]
                + s_got[rank:, :]
                - dot(g_now[rank:, :][:, block], z_own[-1])
                - dot(g_got[rank:, :][:, block], z_sib[-1])
            )
            s_copy = send(s_next, got[height + 1][0], height + 1, 3 * height + 3)
            sends.append(s_copy)
            k_copy.wait_recv()
            k_next[...] = k_now[rank:, :] + k_got[rank:, :]
            k_copy = send(k_next, got[height + 1][2], height + 1, 3 * height + 5)
            sends.append(k_copy)
            g_copy = advance_gram(height + 1, g_copy)
    rows = levels * rank
    scale = 1.0 / math.sqrt(cols)
    z_all = jnp.concatenate(z_own, 0)
    areas = [pl.ds(n * rows, rows) for n in range(3)]
    packed[:rank, :] = z_sib[0]
    packed[rank:rows, :] = z_all[rank:]
    last = [send(packed.at[areas[0]], other.at[areas[0]], 0, 3 * levels)]
    z_out[:, keep] = z_all
    l_first = (s_ref[:rank, keep] - dot(g_ref[:rank, :], z_all)) * scale
    packed[rows : rows + rank, :] = l_first
    for height in range(levels):
        shift = rank * height - rank * height // 128 * 128
        part = slice(height * rank, (height + 1) * rank)
        chain = jnp.concatenate([z_sib[height]] + z_own[height + 1 :], 0)
        row = got[height][1][:rank, :][:, shift:]
        l_part = (got[height][0][:rank, :] - dot(row, chain)) * scale
        l_out[part, keep] = l_part
        if height > 0:
            packed[rows + height * rank : rows + (height + 1) * rank, :] = l_part
    last.append(send(packed.at[areas[1]], other.at[areas[1]], 0, 3 * levels + 1))
    k_copy.wait_recv()
    packed[2 * rows : 2 * rows + rank, :] = k_ref[:rank, keep] * scale
    for height in range(levels):
        part = slice(height * rank, (height + 1) * rank)
        k_part = got[height][2][:rank, :] * scale
        k_out[part, keep] = k_part
        if height > 0:
            packed[2 * rows + height * rank : 2 * rows + (height + 1) * rank, :] = k_part
    last.append(send(packed.at[areas[2]], other.at[areas[2]], 0, 3 * levels + 2))
    for copy, target, area in zip(last, (z_out, l_out, k_out), areas):
        copy.wait_recv()
        target[:, give] = other[area, :]
    for copy in sends + last:
        copy.wait_send()


def tree_scratch(levels, rank, rows, cols, node_shape):
    half = cols // 2
    own, got = [], []
    for height in range(levels):
        left = rows - rank * height
        wide = rows - rank * height // 128 * 128
        group = [
            pltpu.VMEM((left, half), jnp.float32),
            pltpu.VMEM((left, wide), jnp.float32),
            pltpu.VMEM((left, half), jnp.float32),
        ]
        got += group
        if height > 0:
            own += group
    count = 4 * levels + 1
    return (
        [pltpu.VMEM((levels,) + node_shape, jnp.float32)]
        + own
        + got
        + [
            pltpu.VMEM((3 * rows, half), jnp.float32),
            pltpu.VMEM((3 * rows, half), jnp.float32),
            pltpu.SemaphoreType.DMA((levels,)),
            pltpu.SemaphoreType.DMA((count,)),
            pltpu.SemaphoreType.DMA((count,)),
        ]
    )


def tree(sums, weight_sums, gram, node_inverse, levels, rank, base):
    rows, cols = sums.shape
    vmem = pl.BlockSpec(memory_space=pltpu.VMEM)
    return pl.pallas_call(
        functools.partial(tree_kernel, levels, rank, base),
        out_shape=[jax.ShapeDtypeStruct((rows, cols), jnp.float32)] * 3,
        in_specs=[vmem] * 3 + [pl.BlockSpec(memory_space=pl.ANY)],
        out_specs=[vmem] * 3,
        scratch_shapes=tree_scratch(levels, rank, rows, cols, node_inverse.shape[1:]),
        compiler_params=pltpu.CompilerParams(collective_id=0, has_side_effects=True),
    )(sums, weight_sums, gram, node_inverse)


def whole_tree(leaf_rows, right_side, cotangent, basis, saved, node_inverse, levels, rank, tile):
    rows, depth = basis.shape
    cols = right_side.shape[1]
    vmem = pl.BlockSpec(memory_space=pltpu.VMEM)
    hbm = pl.BlockSpec(memory_space=pltpu.HBM)
    args = (right_side, cotangent, basis, saved, node_inverse)
    shapes = (
        [((rows, cols), jnp.float32)] * 2
        + [((depth, cols), jnp.float32)]
        + [((depth, cols), jnp.bfloat16)] * 2
    )
    return pl.pallas_call(
        functools.partial(whole_kernel, levels, rank, tile),
        out_shape=[pltpu.VMEM(shape, dtype) for shape, dtype in shapes],
        in_specs=[pl.BlockSpec(memory_space=pltpu.SMEM)] + [hbm] * 5,
        out_specs=[vmem] * 5,
        scratch_shapes=whole_scratch(levels, rank, rows, cols, depth, depth // tile),
        compiler_params=pltpu.CompilerParams(
            collective_id=0, has_side_effects=True, vmem_limit_bytes=VMEM_TREE
        ),
    )(leaf_rows, *[pltpu.with_memory_space_constraint(arg, pltpu.HBM) for arg in args])


def whole_scratch(levels, rank, rows, cols, depth, tiles):
    half, pairs = cols // 2, 2 * rank

    def full(*shape):
        return pltpu.VMEM(shape, jnp.float32)

    def short(*shape):
        return pltpu.VMEM(shape, jnp.bfloat16)

    steps = [full(rows - rank * height, half) for height in range(levels)]
    return (
        [full(rows, cols), short(rows, depth), short(rows, depth)]
        + [full(rows, cols), full(rows, cols), full(rows, rows), full(rows, rows)]
        + [full(depth, cols)]
        + [full(rows, depth)] * 2
        + [short(rows, depth)] * 2
        + [full(levels, pairs, pairs)]
        + [short(pairs + rows + pairs, pairs)] * 2
        + [full(rank, half)]
        + [full(rows, half)] * 3
        + [
            pltpu.SemaphoreType.DMA((4, tiles)),
            pltpu.SemaphoreType.DMA((levels,)),
            pltpu.SemaphoreType.DMA((SLOTS,)),
            pltpu.SemaphoreType.DMA((SLOTS,)),
        ]
        + steps * 4
        + [
            full(rows - rank, rows),
            full(rows - rank, pairs),
            full(rows - rank, pairs),
            full(pairs, pairs),
            full(pairs, pairs),
            full(rank, pairs),
            full(rank, pairs),
            full(2, rank, pairs),
            full(2, rank, half),
        ]
    )


def finish_kernel(
    tile,
    rows_ref,
    l_ref,
    k_ref,
    x_ref,
    cot_high,
    cot_low,
    x_hbm,
    left_hbm,
    grad_hbm,
    left_ref,
    grad_ref,
    sem,
):
    tiles = x_ref.shape[0] // tile
    copies = []

    def out(source, target, index, kind, n):
        copy = pltpu.make_async_copy(source.at[index], target.at[index], sem.at[kind, n])
        copy.start()
        copies.append(copy)

    left, right = split(l_ref[...]), split(k_ref[...])
    for n in range(tiles):
        out(x_ref, x_hbm, (slice(n * tile, (n + 1) * tile), slice(None)), 0, n)
    for n in range(tiles):
        part = slice(n * tile, (n + 1) * tile)
        down, across = (part, slice(None)), (slice(None), part)
        value = triple(left, (cot_high[down], cot_low[down]), ((1,), (1,)))
        live = n * tile + lax.broadcasted_iota(jnp.int32, (1, tile), 1) < rows_ref[0]
        left_ref[across] = jnp.where(live, value, 0.0).astype(jnp.bfloat16)
        out(left_ref, left_hbm, across, 1, n)
        value = triple(right, split(x_ref[down]), ((1,), (1,)))
        grad_ref[across] = value.astype(jnp.bfloat16)
        out(grad_ref, grad_hbm, across, 2, n)
    for copy in copies:
        copy.wait()


def finish(leaf_rows, parts, tile):
    depth, cols = parts[2].shape
    rows = parts[0].shape[0]
    vmem = pl.BlockSpec(memory_space=pltpu.VMEM)
    hbm = pl.BlockSpec(memory_space=pltpu.HBM)
    shapes = [
        ((depth, cols), jnp.float32),
        ((rows, depth), jnp.bfloat16),
        ((rows, depth), jnp.bfloat16),
    ]
    return pl.pallas_call(
        functools.partial(finish_kernel, tile),
        out_shape=[pltpu.HBM(shape, dtype) for shape, dtype in shapes],
        in_specs=[pl.BlockSpec(memory_space=pltpu.SMEM)] + [vmem] * 5,
        out_specs=[hbm] * 3,
        scratch_shapes=[pltpu.VMEM(shape, dtype) for shape, dtype in shapes[1:]]
        + [pltpu.SemaphoreType.DMA((3, depth // tile))],
        compiler_params=pltpu.CompilerParams(vmem_limit_bytes=VMEM_FINISH),
    )(leaf_rows, *[pltpu.with_memory_space_constraint(part, pltpu.VMEM) for part in parts])


def split(value):
    high = value.astype(jnp.bfloat16)
    return high, (value - high.astype(jnp.float32)).astype(jnp.bfloat16)


def triple(left, right, dims):
    def one(a, b):
        return lax.dot_general(a, b, (dims, ((), ())), preferred_element_type=jnp.float32)

    return one(left[0], right[1]) + one(left[1], right[0]) + one(left[0], right[0])


def lead_kernel(rows_ref, right_ref, cot_ref, basis_ref, saved_ref, s_ref, k_ref, g_ref):
    step = pl.program_id(0)
    tile = basis_ref.shape[1]
    place = step * tile + lax.broadcasted_iota(jnp.int32, (1, tile), 1)
    basis = split(jnp.where(place < rows_ref[0], basis_ref[...], 0.0))
    s_now = triple(basis, split(right_ref[...]), ((1,), (0,)))
    k_now = triple(basis, split(cot_ref[...]), ((1,), (0,)))
    g_now = triple(basis, split(saved_ref[...]), ((1,), (1,)))

    @pl.when(step == 0)
    def _():
        s_ref[...] = s_now
        k_ref[...] = k_now
        g_ref[...] = g_now

    @pl.when(step > 0)
    def _():
        s_ref[...] += s_now
        k_ref[...] += k_now
        g_ref[...] += g_now


def close_kernel(
    rows_ref, right_ref, cot_ref, saved_ref, z_ref, l_ref, k_ref, x_ref, left_ref, grad_ref
):
    tile = saved_ref.shape[1]
    first = pl.program_id(0) * tile
    down = first + lax.broadcasted_iota(jnp.int32, (tile, 1), 0)
    across = first + lax.broadcasted_iota(jnp.int32, (1, tile), 1)
    moved = triple(split(saved_ref[...]), split(z_ref[...]), ((0,), (0,)))
    solved = jnp.where(down < rows_ref[0], right_ref[...] - moved, 0.0)
    x_ref[...] = solved
    left = triple(split(l_ref[...]), split(cot_ref[...]), ((1,), (1,)))
    left_ref[...] = jnp.where(across < rows_ref[0], left, 0.0).astype(jnp.bfloat16)
    grad = triple(split(k_ref[...]), split(solved), ((1,), (1,)))
    grad_ref[...] = grad.astype(jnp.bfloat16)


def body(right_side, cotangent, coeff_basis, saved_basis, node_inverse, leaf_rows):
    row_count, cols = right_side.shape
    levels, rank = coeff_basis.shape[0], coeff_basis.shape[1]
    height = levels * rank
    base = lax.axis_size("leaf").bit_length() - 1 - levels
    basis = coeff_basis.reshape(height, row_count)
    saved = saved_basis.reshape(height, row_count)
    tile = math.gcd(row_count, TILE)
    grid = (row_count // tile,)
    count = pl.BlockSpec(memory_space=pltpu.SMEM)
    tall = pl.BlockSpec((tile, cols), lambda i: (i, 0))
    wide = pl.BlockSpec((height, tile), lambda i: (0, i))
    small = pl.BlockSpec((height, cols), lambda i: (0, 0))
    square = pl.BlockSpec((height, height), lambda i: (0, 0))
    if base == 0:
        parts = whole_tree(
            leaf_rows, right_side, cotangent, basis, saved, node_inverse, levels, rank, tile
        )
        current, left, right = finish(leaf_rows, parts, tile // 2)
    else:
        sums, weight_sums, gram = pl.pallas_call(
            lead_kernel,
            grid=grid,
            out_shape=[
                jax.ShapeDtypeStruct((height, cols), jnp.float32),
                jax.ShapeDtypeStruct((height, cols), jnp.float32),
                jax.ShapeDtypeStruct((height, height), jnp.float32),
            ],
            in_specs=[count, tall, tall, wide, wide],
            out_specs=[small, small, square],
        )(leaf_rows, right_side, cotangent, basis, saved)
        for bit in range(base):
            sums = sums + swapped(sums, bit)
            weight_sums = weight_sums + swapped(weight_sums, bit)
            gram = gram + swapped(gram, bit)
        z_own, l_sib, k_sib = tree(sums, weight_sums, gram, node_inverse, levels, rank, base)
        current, left, right = pl.pallas_call(
            close_kernel,
            grid=grid,
            out_shape=[
                jax.ShapeDtypeStruct((row_count, cols), jnp.float32),
                jax.ShapeDtypeStruct((height, row_count), jnp.bfloat16),
                jax.ShapeDtypeStruct((height, row_count), jnp.bfloat16),
            ],
            in_specs=[count, tall, tall, wide, small, small, small],
            out_specs=[tall, wide, wide],
        )(leaf_rows, right_side, cotangent, saved, z_own, l_sib, k_sib)
    shape = (levels, rank, row_count)
    return current, left.reshape(shape), right.reshape(shape)


def solution(mesh):
    in_specs = (
        P(("groups", "leaf"), None),
        P(("groups", "leaf"), None),
        P(None, None, ("groups", "leaf")),
        P(None, None, ("groups", "leaf")),
        P("groups", None, None),
        P(("groups", "leaf")),
    )
    out_specs = (
        P(("groups", "leaf"), None),
        P(None, None, ("groups", "leaf")),
        P(None, None, ("groups", "leaf")),
    )
    return jax.shard_map(body, mesh=mesh, in_specs=in_specs, out_specs=out_specs, check_vma=False)
```
